32 devices in a mesh: dp: 4 (over y, core), expert: 8 (over z, x).
Axes of the slice: x: 2, y: 2, z: 4, core: 2. Of those that a mesh axis runs over, the one named last changes fastest.
Arguments:
- latents: bfloat16 [4096, 2048], P(('dp', 'expert')), may hold values from -6 to 6
- expert_ids: int32 [4096, 6], P(('dp', 'expert')), may hold values from 0 to 31, as said below
- gate_weights: float32 [4096, 6], P(('dp', 'expert')), may hold values from 0.05 to 0.5
- capacity: int32 [4, 32], P('dp'), may hold values from 12 to 24, as said below
- hot_expert: int32 [4], P('dp'), may hold values from 0 to 31
- w_gate: bfloat16 [32, 2048, 704], P('expert'), may hold values from -0.125 to 0.125
- w_up: bfloat16 [32, 2048, 704], P('expert'), may hold values from -0.125 to 0.125
- w_down: bfloat16 [32, 704, 2048], P('expert'), may hold values from -0.21875 to 0.21875
- shared_gate: bfloat16 [2048, 2048], P(None, 'dp'), may hold values from -0.125 to 0.125
- shared_up: bfloat16 [2048, 2048], P(None, 'dp'), may hold values from -0.125 to 0.125
- shared_down: bfloat16 [2048, 2048], P('dp'), may hold values from -0.125 to 0.125
Outputs:
- mixed: bfloat16 [4096, 2048], P(('dp', 'expert'))
The draws below stay inside these ranges and needn't reach their ends.
Inputs may be any that keep to these rules, and one draw needn't show every extreme that they name: `expert_ids`: A token names 6 different experts. In every block of 128 token rows the hot expert of the block's data group is named in exactly 40 assignments, and every other expert in at most 24. `capacity`: each data group's row holds the value 24 in at least one column.
All inputs are finite; a program needn't handle non-finite values.
Results may differ from the reference program's by a relative error of at most 0.0095.
Values may be sent and summed in bfloat16 or wider, within the bound.
No kernel may reach another device: no remote copies, remote signals or barrier semaphores. Data moves between devices by JAX's collectives and lax.ppermute only.
A program may use at most 128 MiB of HBM per device.

```python
import math
import jax
import jax.numpy as jnp
from jax import lax

D = 2048
FF = 704
SH = 2048
E = 32
K = 6
TOK_DEV = 128
CAP = 40
CAP_COLD = 24
TOKENS = 4096
N_DP = 4
N_EXPERT = 8


def hot_of_groups(key):
    first, second = jax.random.split(jax.random.fold_in(key, 5))
    values = jax.random.randint(first, (N_DP,), 0, E).astype(jnp.int32)
    order = jax.random.permutation(second, N_DP).astype(jnp.int32)
    values = values.at[order[0]].set(0)
    values = values.at[order[1]].set(E - 1)
    return values.astype(jnp.int32)


def draw_hot_expert(key, part):
    return hot_of_groups(key)


def route_block(block_key, hot):
    keys = jax.random.split(block_key, 4)
    has_hot = (jax.random.permutation(keys[0], TOK_DEV) < CAP).astype(jnp.int32)
    counts = K - has_hot
    order = jax.random.permutation(keys[1], TOK_DEV)
    in_order = counts[order]
    before = jnp.cumsum(in_order) - in_order
    offset = jnp.zeros((TOK_DEV,), jnp.int32).at[order].set(before.astype(jnp.int32))
    shuffled = jax.random.permutation(keys[2], E).astype(jnp.int32)
    moved = jnp.argsort((shuffled == hot).astype(jnp.int32), stable=True)
    others = shuffled[moved][:E - 1]
    columns = jnp.arange(K, dtype=jnp.int32)
    picks = others[(offset[:, None] + columns[None, :]) % (E - 1)]
    rows = jnp.where((has_hot[:, None] == 1) & (columns[None, :] == K - 1), hot, picks)
    mixing = jax.vmap(lambda row_key: jax.random.permutation(row_key, K))(jax.random.split(keys[3], TOK_DEV))
    return jnp.take_along_axis(rows, mixing.astype(jnp.int32), axis=1).astype(jnp.int32)


def draw_expert_ids(key, part):
    hot = hot_of_groups(key)
    blocks = TOKENS // TOK_DEV
    per_group = blocks // N_DP
    block_index = jnp.arange(blocks, dtype=jnp.int32)
    block_keys = jax.vmap(lambda index: jax.random.fold_in(jax.random.fold_in(key, 9), index))(block_index)
    block_hot = hot[block_index // per_group]
    routes = jax.vmap(route_block)(block_keys, block_hot)
    return routes.reshape(TOKENS, K).astype(jnp.int32)


def draw_capacity(key, part):
    first, second = jax.random.split(jax.random.fold_in(key, 17))
    values = jax.random.randint(first, (N_DP, E), max(1, CAP_COLD // 2), CAP_COLD + 1)
    where_full = jax.random.randint(second, (N_DP, 1), 0, E)
    columns = jnp.arange(E, dtype=jnp.int32)[None, :]
    return jnp.where(columns == where_full, CAP_COLD, values).astype(jnp.int32)


def block_levels(rng, dims, shards, smallest, top_value):
    gain = 1.0
    for axis_at, parts in shards:
        steps = jax.random.uniform(jax.random.fold_in(jax.random.fold_in(rng, 6), axis_at), (parts,), jnp.float32, smallest / len(shards), top_value / len(shards))
        gain = gain * jnp.repeat(jnp.exp(steps), dims[axis_at] // parts).reshape((-1,) + (1,) * (len(dims) - 1 - axis_at))
    return gain


def noise(own_key, dims, deviation, most, cuts=(), kind=jnp.bfloat16):
    entries = jax.random.normal(own_key, dims, jnp.float32) * deviation
    if len(cuts) > 0:
        entries = block_levels(own_key, dims, cuts, -0.22, 0.18) * entries
    return jnp.clip(entries, min=-most, max=most).astype(kind)


def setup_inputs(seed: int = 0) -> dict:
    key_of = jax.random.split(jax.random.key(seed), 12)
    latents = noise(key_of[0], (TOKENS, D), 1.0, 6.0, ((0, 32),))
    expert_ids = draw_expert_ids(jax.random.fold_in(key_of[11], 71), 0)
    gate_weights = jnp.clip(jnp.exp(math.log(0.5) - 2.3025851 * jax.random.uniform(key_of[2], (TOKENS, K), jnp.float32) ** block_levels(key_of[2], (TOKENS, K), ((0, 32),), -0.2, 0.2)), 0.05, 0.5)
    capacity = draw_capacity(jax.random.fold_in(key_of[11], 71), 0)
    hot_expert = draw_hot_expert(jax.random.fold_in(key_of[11], 71), 0)
    w_gate = noise(key_of[5], (E, D, FF), D ** -0.5, 0.125, ((0, 8),))
    w_up = noise(key_of[6], (E, D, FF), D ** -0.5, 0.125, ((0, 8),))
    w_down = noise(key_of[7], (E, FF, D), FF ** -0.5, 0.21875, ((0, 8),))
    shared_gate = noise(key_of[8], (D, SH), D ** -0.5, 0.125, ((1, 4),))
    shared_up = noise(key_of[9], (D, SH), D ** -0.5, 0.125, ((1, 4),))
    shared_down = noise(key_of[10], (SH, D), SH ** -0.5, 0.125, ((0, 4),))
    return {"latents": latents, "expert_ids": expert_ids, "gate_weights": gate_weights, "capacity": capacity, "hot_expert": hot_expert, "w_gate": w_gate, "w_up": w_up, "w_down": w_down, "shared_gate": shared_gate, "shared_up": shared_up, "shared_down": shared_down}


def expert_rows(rows, first, second, third):
    gate = jnp.dot(rows, first, preferred_element_type=jnp.float32)
    upper = jnp.dot(rows, second, preferred_element_type=jnp.float32)
    hidden = (jax.nn.silu(gate) * upper).astype(jnp.bfloat16)
    return jnp.dot(hidden, third, preferred_element_type=jnp.float32).astype(jnp.bfloat16)


def reference(latents, expert_ids, gate_weights, capacity, hot_expert, w_gate, w_up, w_down, shared_gate, shared_up, shared_down):
    ndevs = N_DP * N_EXPERT
    assign = TOK_DEV * K
    flat = expert_ids.reshape(ndevs, assign)
    gates = gate_weights.reshape(ndevs, assign)
    group = jnp.arange(ndevs, dtype=jnp.int32) // N_EXPERT
    cap_rows = capacity[group]
    hot_rows = hot_expert[group]
    labels = jnp.arange(E, dtype=jnp.int32)
    limit = jnp.where(labels[None, :] == hot_rows[:, None], CAP, cap_rows)
    onehot = (flat[:, :, None] == labels[None, None, :]).astype(jnp.int32)
    rank = jnp.sum((jnp.cumsum(onehot, axis=1) - onehot) * onehot, axis=2)
    bound = jnp.take_along_axis(limit, flat, axis=1)
    kept = rank < bound
    slot = jnp.where(kept, flat * CAP + rank, E * CAP).astype(jnp.int32)
    token_of = (jnp.arange(assign, dtype=jnp.int32) // K).astype(jnp.int32)

    def fill_table(slots, gate_row):
        table = jnp.full((E * CAP + 1,), TOK_DEV, jnp.int32).at[slots].set(token_of)
        weight = jnp.zeros((E * CAP + 1,), jnp.float32).at[slots].set(gate_row)
        return table[:E * CAP], weight[:E * CAP]

    table, weight = jax.vmap(fill_table)(slot, gates)
    table = table.reshape(ndevs, E, CAP).transpose(1, 0, 2)
    weight = weight.reshape(ndevs, E, CAP).transpose(1, 0, 2)
    padded = jnp.concatenate([latents.reshape(ndevs, TOK_DEV, D), jnp.zeros((ndevs, 1, D), jnp.bfloat16)], axis=1)
    device_of = jnp.arange(ndevs, dtype=jnp.int32)[:, None]

    def step(carry, items):
        tbl, wgt, first, second, third = items
        rows = padded[device_of, tbl]
        out = expert_rows(rows.reshape(ndevs * CAP, D), first, second, third).reshape(ndevs, CAP, D)
        carry = carry.at[device_of, tbl].add(wgt[:, :, None] * out.astype(jnp.float32))
        return carry, None

    routed0 = jnp.zeros((ndevs, TOK_DEV + 1, D), jnp.float32)
    routed, _ = lax.scan(step, routed0, (table, weight, w_gate, w_up, w_down))
    routed = routed[:, :TOK_DEV, :].reshape(TOKENS, D)
    slice_width = SH // N_DP
    shared = jnp.zeros((TOKENS, D), jnp.float32)
    for index in range(N_DP):
        lo = index * slice_width
        term = expert_rows(latents, shared_gate[:, lo:lo + slice_width], shared_up[:, lo:lo + slice_width], shared_down[lo:lo + slice_width, :])
        shared = shared + term.astype(jnp.float32)
    return (shared + routed).astype(jnp.bfloat16)
```

```python
import functools

import jax
import jax.numpy as jnp
from jax import lax
from jax.experimental import pallas as pl
from jax.experimental.pallas import tpu as pltpu
from jax.sharding import PartitionSpec as P

HOT_SLOTS = 40
SLOTS = 24
EXTRA = HOT_SLOTS - SLOTS
BF16 = jnp.bfloat16
F32 = jnp.float32
ANY = pl.BlockSpec(memory_space=pl.ANY)
VMEM = pl.BlockSpec(memory_space=pltpu.VMEM)
SMEM = pl.BlockSpec(memory_space=pltpu.SMEM)


def ring_of(count):
    return list(range(0, count, 2)) + list(range(count - 1, 0, -2))


def offsets_of(count):
    order = [0, count // 2]
    for hop in range(1, count // 2):
        order += [hop, count - hop]
    return order


def dot(a, b):
    return jnp.dot(a, b, preferred_element_type=F32)


def routing(expert_ids, gate_weights, capacity, hot_expert, experts):
    tokens, top = expert_ids.shape
    ids, gates = expert_ids.T, gate_weights.T
    labels = jnp.arange(experts, dtype=jnp.int32)[:, None]
    chosen = jnp.zeros((experts, tokens), jnp.bool_)
    weight = jnp.zeros((experts, tokens), F32)
    for k in range(top):
        here = ids[k][None, :] == labels
        chosen = chosen | here
        weight = weight + jnp.where(here, gates[k][None, :], 0.0)
    place = jnp.arange(tokens, dtype=jnp.int32)
    earlier = (place[:, None] < place[None, :]).astype(BF16)
    rank = dot(chosen.astype(BF16), earlier)
    limit = jnp.where(labels == hot_expert[0], HOT_SLOTS, capacity[0][:, None]).astype(F32)
    kept = chosen & (rank < limit)
    return jnp.stack([jnp.where(kept, rank, -1.0), jnp.where(kept, weight, 0.0)], axis=1)


def experts_kernel(count, local, idx, meta, *refs):
    half = 64
    pairs = count // 2
    offsets = offsets_of(count)
    units = {}
    at = 0
    for o in range(count):
        units[o] = refs[at : at + (1 if o == 0 else 2)]
        at += len(units[o])
    w_gate, w_up, w_down = refs[at : at + 3]
    at += 3
    outs = [refs[at + 2 * o : at + 2 * o + 2] for o in range(count)]
    at += 2 * count
    x, wg, wu, wd, rows, rows_x, eo, sel, scale, scale_x, sem_x, sem_w, sem_o = refs[at:]
    wide = 2 * SLOTS
    wide_x = 2 * EXTRA
    hot = idx[count]

    loads = []
    for slot, o in enumerate(offsets):
        mine = []
        for h, unit in enumerate(units[o]):
            length = unit.shape[0]
            copy = pltpu.make_async_copy(unit, x.at[slot, pl.ds(h * length, length)], sem_x.at[slot, h])
            copy.start()
            mine.append(copy)
        loads.append(mine)
    weights = []
    for e in range(local):
        mine = []
        for k, (source, target) in enumerate(((w_gate, wg), (w_up, wu), (w_down, wd))):
            copy = pltpu.make_async_copy(source.at[e], target.at[e], sem_w.at[e, k])
            copy.start()
            mine.append(copy)
        weights.append(mine)

    lane = lax.broadcasted_iota(jnp.int32, (1, 256), 1)
    second = (lane >= 128).astype(F32)
    for p in range(pairs):
        for slot in (2 * p, 2 * p + 1):
            for copy in loads[slot]:
                copy.wait()
        info = [meta[idx[offsets[2 * p + i]]] for i in range(2)]
        blocks = []
        for e in range(local):
            rank = jnp.concatenate([info[0][2 * e : 2 * e + 1], info[1][2 * e : 2 * e + 1]], axis=1)
            gate = jnp.concatenate([info[0][2 * e + 1 : 2 * e + 2], info[1][2 * e + 1 : 2 * e + 2]], axis=1)
            key = jnp.where((rank >= 0) & (rank < SLOTS), rank + SLOTS * second, -1.0).astype(jnp.int32)
            pick = (lax.broadcasted_iota(jnp.int32, (wide, 256), 0) == key).astype(F32)
            blocks.append(pick)
            scale[e, pl.ds(p * wide, wide), :] = jnp.broadcast_to(
                jnp.sum(pick * gate, axis=1, keepdims=True), (wide, 128)
            )
            here = hot == e
            key_x = jnp.where((rank >= SLOTS) & here, rank - SLOTS + EXTRA * second, -1.0).astype(jnp.int32)
            pick_x = (lax.broadcasted_iota(jnp.int32, (wide_x, 256), 0) == key_x).astype(F32)
            gate_x = jnp.sum(pick_x * gate, axis=1, keepdims=True)
            if e == 0:
                extra, extra_gate = pick_x, gate_x
            else:
                extra, extra_gate = extra + pick_x, extra_gate + gate_x
        scale_x[pl.ds(p * wide_x, wide_x), :] = jnp.broadcast_to(extra_gate, (wide_x, 128))
        blocks.append(extra)
        pick = jnp.concatenate(blocks, axis=0).astype(BF16)
        sel[p] = pick
        pair = x[2 * p : 2 * p + 2].reshape(256, x.shape[2])
        got = dot(pick, pair).astype(BF16)
        for e in range(local):
            rows[e, pl.ds(p * wide, wide), :] = got[e * wide : (e + 1) * wide]
        rows_x[pl.ds(p * wide_x, wide_x), :] = got[local * wide :]
        eo[p, pl.ds(local * wide, wide_x), :] = jnp.zeros((wide_x, x.shape[2]), BF16)

    def hidden_of(e, tokens, weight):
        gate = dot(tokens, wg[e])
        upper = dot(tokens, wu[e])
        return (gate / (1.0 + jnp.exp(-gate)) * upper * weight).astype(BF16)

    for e in range(local):
        weights[e][0].wait()
        weights[e][1].wait()
        hidden = hidden_of(e, rows[e], scale[e][:, :1])
        weights[e][2].wait()
        out = dot(hidden, wd[e]).astype(BF16)
        for p in range(pairs):
            eo[p, pl.ds(e * wide, wide), :] = out[p * wide : (p + 1) * wide]

        @pl.when(hot == e)
        def _():
            more = dot(hidden_of(e, rows_x[...], scale_x[...][:, :1]), wd[e]).astype(BF16)
            for p in range(pairs):
                eo[p, pl.ds(local * wide, wide_x), :] = more[p * wide_x : (p + 1) * wide_x]

    stores = []
    for p in range(pairs):
        total = lax.dot_general(sel[p], eo[p], (((0,), (0,)), ((), ())), preferred_element_type=F32)
        x[2 * p : 2 * p + 2] = total.astype(BF16).reshape(2, 128, x.shape[2])
        for slot in (2 * p, 2 * p + 1):
            for h in range(2):
                copy = pltpu.make_async_copy(
                    x.at[slot, pl.ds(h * half, half)], outs[offsets[slot]][h], sem_o.at[slot, h]
                )
                copy.start()
                stores.append(copy)
    for copy in stores:
        copy.wait()


def run_experts(count, local, idx, meta, blocks, w_gate, w_up, w_down):
    width, hidden = w_gate.shape[1:]
    wide, wide_x = 2 * SLOTS, 2 * EXTRA
    pairs = count // 2
    high = local * wide + wide_x
    flat = [unit for o in range(count) for unit in blocks[o]]
    flops = 2 * 3 * width * hidden * count * (local * SLOTS + EXTRA) + 4 * count * 128 * high * width
    return pl.pallas_call(
        functools.partial(experts_kernel, count, local),
        out_shape=[jax.ShapeDtypeStruct((64, width), BF16)] * (2 * count),
        in_specs=[SMEM, VMEM] + [ANY] * (len(flat) + 3),
        out_specs=[ANY] * (2 * count),
        scratch_shapes=[
            pltpu.VMEM((count, 128, width), BF16),
            pltpu.VMEM((local, width, hidden), BF16),
            pltpu.VMEM((local, width, hidden), BF16),
            pltpu.VMEM((local, hidden, width), BF16),
            pltpu.VMEM((local, pairs * wide, width), BF16),
            pltpu.VMEM((pairs * wide_x, width), BF16),
            pltpu.VMEM((pairs, high, width), BF16),
            pltpu.VMEM((pairs, high, 256), BF16),
            pltpu.VMEM((local, pairs * wide, 128), F32),
            pltpu.VMEM((pairs * wide_x, 128), F32),
            pltpu.SemaphoreType.DMA((count, 2)),
            pltpu.SemaphoreType.DMA((local, 3)),
            pltpu.SemaphoreType.DMA((count, 2)),
        ],
        cost_estimate=pl.CostEstimate(
            flops=flops,
            transcendentals=count * local * SLOTS * hidden,
            bytes_accessed=2 * (3 * local * width * hidden + 2 * count * 128 * width),
        ),
        compiler_params=pltpu.CompilerParams(vmem_limit_bytes=60 << 20),
        name="routed_experts",
    )(idx, meta, *flat, w_gate, w_up, w_down)


def shared_kernel(first, second, w_gate, w_up, w_down, out_first, out_second):
    tokens = jnp.concatenate([first[...], second[...]], axis=0)
    gate = dot(tokens, w_gate[...])
    upper = dot(tokens, w_up[...])
    hidden = (gate / (1.0 + jnp.exp(-gate)) * upper).astype(BF16)
    out = dot(hidden, w_down[...]).astype(BF16)
    rows = first.shape[0]
    out_first[...] = out[:rows]
    out_second[...] = out[rows:]


def run_shared(first, second, w_gate, w_up, w_down):
    rows, width = first.shape
    hidden = w_gate.shape[1]
    return pl.pallas_call(
        shared_kernel,
        out_shape=[jax.ShapeDtypeStruct((rows, width), BF16)] * 2,
        in_specs=[VMEM] * 5,
        out_specs=[VMEM] * 2,
        cost_estimate=pl.CostEstimate(
            flops=2 * 3 * 2 * rows * width * hidden,
            transcendentals=2 * rows * hidden,
            bytes_accessed=2 * (3 * width * hidden + 4 * rows * width),
        ),
        compiler_params=pltpu.CompilerParams(vmem_limit_bytes=48 << 20),
        name="shared_experts",
    )(first, second, w_gate, w_up, w_down)


def on_device(
    latents,
    expert_ids,
    gate_weights,
    capacity,
    hot_expert,
    w_gate,
    w_up,
    w_down,
    shared_gate,
    shared_up,
    shared_down,
):
    tokens, width = latents.shape
    half = tokens // 2
    experts = capacity.shape[1]
    local = w_gate.shape[0]
    count = lax.axis_size("expert")
    n_dp = lax.axis_size("dp")
    ring = ring_of(count)
    forward = [(ring[i], ring[(i + 1) % count]) for i in range(count)]
    backward = [(b, a) for a, b in forward]
    mid = count // 2

    own = [latents[:half], latents[half:]]
    blocks = {o: [None, None] for o in range(count)}
    for h in range(2):
        up, down = own[h], own[h]
        for hop in range(1, mid + 1):
            if hop < mid or h == 0:
                up = lax.ppermute(up, "expert", forward)
                blocks[hop][h] = up
            if hop < mid or h == 1:
                down = lax.ppermute(down, "expert", backward)
                blocks[count - hop][h] = down
    blocks[0] = [latents]

    info = routing(expert_ids, gate_weights, capacity, hot_expert, experts)
    meta = lax.all_to_all(
        info.reshape(count, 2 * local, tokens), "expert", split_axis=0, concat_axis=0, tiled=True
    )
    me = lax.axis_index("expert")
    table = []
    for e in range(count):
        at = ring.index(e)
        table.append([ring[(at - o) % count] for o in range(count)])
    idx = jnp.array(table, jnp.int32)[me]
    idx = jnp.concatenate([idx, (hot_expert - me * local).astype(jnp.int32)])

    bits = [1 << b for b in range(n_dp.bit_length() - 1)]
    near = {0: latents}
    for bit in reversed(bits):
        swap = [(d, d ^ bit) for d in range(n_dp)]
        for r in list(near):
            near[r ^ bit] = lax.ppermute(near[r], "dp", swap)
    part = {}
    for r in range(0, n_dp, 2):
        part[r], part[r + 1] = run_shared(near[r], near[r + 1], shared_gate, shared_up, shared_down)
    for bit in bits:
        swap = [(d, d ^ bit) for d in range(n_dp)]
        for r in sorted(part):
            if r & bit:
                came = lax.ppermute(part.pop(r), "dp", swap)
                total = part[r ^ bit].astype(F32) + came.astype(F32)
                part[r ^ bit] = total if len(bits) and bit == bits[-1] else total.astype(BF16)
    shared = part[0]

    flat = run_experts(count, local, idx, meta, blocks, w_gate, w_up, w_down)
    done = {o: [flat[2 * o], flat[2 * o + 1]] for o in range(count)}

    result = []
    for h in range(2):
        pieces = [done[0][h]]
        for step, perm, long in ((-1, forward, h == 0), (1, backward, h == 1)):
            start = mid if long else mid - 1
            acc = done[(step * start) % count][h]
            for k in range(start, 0, -1):
                came = lax.ppermute(acc, "expert", perm)
                if k > 1:
                    acc = (came.astype(F32) + done[(step * (k - 1)) % count][h].astype(F32)).astype(BF16)
            pieces.append(came)
        total = shared[h * half : (h + 1) * half].astype(F32)
        for piece in pieces:
            total = total + piece.astype(F32)
        result.append(total.astype(BF16))
    return jnp.concatenate(result, axis=0)


def solution(mesh):
    placed = (
        P(("dp", "expert"), None),
        P(("dp", "expert"), None),
        P(("dp", "expert"), None),
        P("dp", None),
        P("dp"),
        P("expert", None, None),
        P("expert", None, None),
        P("expert", None, None),
        P(None, "dp"),
        P(None, "dp"),
        P("dp", None),
    )
    return jax.shard_map(
        on_device, mesh=mesh, in_specs=placed, out_specs=P(("dp", "expert"), None), check_vma=False
    )
```

```python
import functools

import jax
import jax.numpy as jnp
from jax import lax
from jax.experimental import pallas as pl
from jax.experimental.pallas import tpu as pltpu
from jax.sharding import PartitionSpec as P

HOT_SLOTS = 40
SLOTS = 24
EXTRA = HOT_SLOTS - SLOTS
BF16 = jnp.bfloat16
F32 = jnp.float32
HBM = pl.BlockSpec(memory_space=pltpu.HBM)
VMEM = pl.BlockSpec(memory_space=pltpu.VMEM)
SMEM = pl.BlockSpec(memory_space=pltpu.SMEM)


def ring_of(count):
    return list(range(0, count, 2)) + list(range(count - 1, 0, -2))


def offsets_of(count):
    order = [0, count // 2]
    for hop in range(1, count // 2):
        order += [hop, count - hop]
    return order


def dot(a, b):
    return jnp.dot(a, b, preferred_element_type=F32)


def dot_t(a, b):
    return lax.dot_general(a, b, (((1,), (1,)), ((), ())), preferred_element_type=F32)


def dot_l(a, b):
    return lax.dot_general(a, b, (((0,), (0,)), ((), ())), preferred_element_type=F32)


def routing(expert_ids, gate_weights, capacity, hot_expert, experts):
    tokens, top = expert_ids.shape
    ids, gates = expert_ids.T, gate_weights.T
    labels = jnp.arange(experts, dtype=jnp.int32)[:, None]
    chosen = jnp.zeros((experts, tokens), jnp.bool_)
    weight = jnp.zeros((experts, tokens), F32)
    for k in range(top):
        here = ids[k][None, :] == labels
        chosen = chosen | here
        weight = weight + jnp.where(here, gates[k][None, :], 0.0)
    place = jnp.arange(tokens, dtype=jnp.int32)
    earlier = (place[:, None] < place[None, :]).astype(BF16)
    rank = dot(chosen.astype(BF16), earlier)
    limit = jnp.where(labels == hot_expert[0], HOT_SLOTS, capacity[0][:, None]).astype(F32)
    kept = chosen & (rank < limit)
    return jnp.stack([jnp.where(kept, rank, -1.0), jnp.where(kept, weight, 0.0)], axis=1)


def experts_kernel(offsets, groups, sizes, fetch, chained, final, idx, meta, *refs):
    refs = list(refs)
    units = [[refs.pop(0) for _ in range(size)] for size in sizes]
    held = [[refs.pop(0) for _ in range(3)] for _ in groups]
    before = [refs.pop(0) for _ in range(2)] if chained else None
    if final:
        outs = [[refs.pop(0) for _ in range(2)] for _ in offsets]
    else:
        sel, eo = refs.pop(0), refs.pop(0)
    if fetch:
        source, held = held[0], [[refs.pop(0) for _ in range(3)]]
    if final:
        sel, eo = refs.pop(0), refs.pop(0)
    x, rows, scale, sem_x, sem_o, sem_w = refs
    experts = [e for group in groups for e in group]

    def fetching(i, k):
        return pltpu.make_async_copy(source[k].at[experts[0] + i], held[0][k].at[i], sem_w.at[i, k])

    pairs = len(offsets) // 2
    width = x.shape[2]
    wide, wide_x = 2 * SLOTS, 2 * EXTRA
    base = pairs * wide
    full = pairs * (wide + wide_x)
    many = len(experts)
    hot = idx[idx.shape[0] - 1]

    loads = []
    for slot, mine in enumerate(units):
        for h, unit in enumerate(mine):
            length = unit.shape[0]
            copy = pltpu.make_async_copy(unit, x.at[slot, pl.ds(h * length, length)], sem_x.at[slot, h])
            copy.start()
            loads.append(copy)
    if fetch:
        for i in range(len(experts)):
            for k in range(3):
                fetching(i, k).start()

    lane = lax.broadcasted_iota(jnp.int32, (1, 256), 1)
    second = (lane >= 128).astype(F32)
    for p in range(pairs):
        info = [meta[idx[offsets[2 * p + i]]] for i in range(2)]
        blocks = []
        for i, e in enumerate(experts):
            rank = jnp.concatenate([info[0][2 * e : 2 * e + 1], info[1][2 * e : 2 * e + 1]], axis=1)
            gate = jnp.concatenate([info[0][2 * e + 1 : 2 * e + 2], info[1][2 * e + 1 : 2 * e + 2]], axis=1)
            key = jnp.where((rank >= 0) & (rank < SLOTS), rank + SLOTS * second, -1.0).astype(jnp.int32)
            pick = (lax.broadcasted_iota(jnp.int32, (wide, 256), 0) == key).astype(F32)
            blocks.append(pick)
            scale[i, pl.ds(p * wide, wide), :] = jnp.broadcast_to(
                jnp.sum(pick * gate, axis=1, keepdims=True), (wide, 128)
            )
            key_x = jnp.where((rank >= SLOTS) & (hot == e), rank - SLOTS + EXTRA * second, -1.0)
            pick_x = (lax.broadcasted_iota(jnp.int32, (wide_x, 256), 0) == key_x.astype(jnp.int32)).astype(F32)
            scale[i, pl.ds(base + p * wide_x, wide_x), :] = jnp.broadcast_to(
                jnp.sum(pick_x * gate, axis=1, keepdims=True), (wide_x, 128)
            )
            extra = pick_x if i == 0 else extra + pick_x
        blocks.append(extra)
        sel[p] = jnp.concatenate(blocks, axis=0).astype(BF16)
        eo[p, pl.ds(many * wide, wide_x), :] = jnp.zeros((wide_x, width), BF16)

    for copy in loads:
        copy.wait()
    for p in range(pairs):
        pair = x[2 * p : 2 * p + 2].reshape(256, width)
        got = dot(sel[p], pair).astype(BF16)
        for i, e in enumerate(experts):
            rows[i, pl.ds(p * wide, wide), :] = got[i * wide : (i + 1) * wide]

            @pl.when(hot == e)
            def _():
                rows[i, pl.ds(base + p * wide_x, wide_x), :] = got[many * wide :]

    def run(at, group, inside, length):
        wg, wu, wd = held[group]
        tokens = rows[at, :length]
        gate = dot_t(tokens, wg[inside])
        upper = dot_t(tokens, wu[inside])
        hidden = (gate / (1.0 + jnp.exp(-gate)) * upper * scale[at, :length][:, :1]).astype(BF16)
        if fetch:
            fetching(inside, 2).wait()
        out = dot(hidden, wd[inside]).astype(BF16)
        for p in range(pairs):
            eo[p, pl.ds(pl.multiple_of(at * wide, wide), wide), :] = out[p * wide : (p + 1) * wide]
            if length > base:
                eo[p, pl.ds(many * wide, wide_x), :] = out[base + p * wide_x : base + (p + 1) * wide_x]

    done = 0
    for group, members in enumerate(groups):

        def body(inside, carry):
            if fetch:
                fetching(inside, 0).wait()
                fetching(inside, 1).wait()

            @pl.when(hot == members[0] + inside)
            def _():
                run(done + inside, group, inside, full)

            @pl.when(hot != members[0] + inside)
            def _():
                run(done + inside, group, inside, base)

            return carry

        lax.fori_loop(0, len(members), body, 0)
        done += len(members)

    if not final:
        return
    stores = []
    for p in range(pairs):
        total = dot_l(sel[p], eo[p])
        if chained:
            total = total + dot_l(before[0][p], before[1][p])
        x[2 * p : 2 * p + 2] = total.astype(BF16).reshape(2, 128, width)
        for slot in (2 * p, 2 * p + 1):
            for h in range(2):
                copy = pltpu.make_async_copy(x.at[slot, pl.ds(h * 64, 64)], outs[slot][h], sem_o.at[slot, h])
                copy.start()
                stores.append(copy)
    for copy in stores:
        copy.wait()


def run_experts(offsets, groups, idx, meta, blocks, weights, fetch=False, before=None, final=True):
    hidden, width = weights[0][2].shape[1:]
    wide, wide_x = 2 * SLOTS, 2 * EXTRA
    pairs = len(offsets) // 2
    many = sum(len(group) for group in groups)
    high = many * wide + wide_x
    full = pairs * (wide + wide_x)
    flat = [unit for o in offsets for unit in blocks[o]]
    sizes = tuple(len(blocks[o]) for o in offsets)
    chain = [((pairs, high, 256), BF16), ((pairs, high, width), BF16)]
    scratch = [
        pltpu.VMEM((len(offsets), 128, width), BF16),
        pltpu.VMEM((many, full, width), BF16),
        pltpu.VMEM((many, full, 128), F32),
        pltpu.SemaphoreType.DMA((len(offsets), 2)),
        pltpu.SemaphoreType.DMA((len(offsets), 2)),
        pltpu.SemaphoreType.DMA((many, 3)),
    ]
    if final:
        out_shape = [pltpu.HBM((64, width), BF16)] * (2 * len(offsets))
        out_specs = [HBM] * (2 * len(offsets))
        scratch = [pltpu.VMEM(*c) for c in chain] + scratch
    else:
        out_shape = [pltpu.VMEM(*c) for c in chain]
        out_specs = [VMEM] * 2
    if fetch:
        out_shape = out_shape + [pltpu.VMEM((many, hidden, width), BF16)] * 3
        out_specs = out_specs + [VMEM] * 3
    flat = [pltpu.with_memory_space_constraint(unit, pltpu.HBM) for unit in flat]
    room = len(offsets) * 128 * width * 2 + many * full * (2 * width + 512) + pairs * high * (2 * width + 512)
    room += full * (6 * width + 10 * hidden)
    before = list(before or ())
    held = [w for group in weights for w in group]
    held = [pltpu.with_memory_space_constraint(w, pltpu.HBM if fetch else pltpu.VMEM) for w in held]
    before = [pltpu.with_memory_space_constraint(w, pltpu.VMEM) for w in before]
    flops = 2 * 3 * width * hidden * many * pairs * wide + 4 * len(offsets) * 128 * high * width
    return pl.pallas_call(
        functools.partial(experts_kernel, offsets, groups, sizes, fetch, bool(before), final),
        out_shape=out_shape,
        in_specs=[SMEM, VMEM] + [HBM] * len(flat) + [HBM if fetch else VMEM] * len(held) + [VMEM] * len(before),
        out_specs=out_specs,
        scratch_shapes=scratch,
        cost_estimate=pl.CostEstimate(
            flops=flops,
            transcendentals=many * pairs * wide * hidden,
            bytes_accessed=2 * (2 * len(offsets) * 128 * width + (3 * many * hidden * width if fetch else 0)),
        ),
        compiler_params=pltpu.CompilerParams(vmem_limit_bytes=room),
        name="routed_experts",
    )(idx, meta, *flat, *held, *before)


def shared_kernel(first, second, w_gate, w_up, w_down, out_first, out_second):
    tokens = jnp.concatenate([first[...], second[...]], axis=0)
    gate = dot(tokens, w_gate[...])
    upper = dot(tokens, w_up[...])
    hidden = (gate / (1.0 + jnp.exp(-gate)) * upper).astype(BF16)
    out = dot(hidden, w_down[...]).astype(BF16)
    rows = first.shape[0]
    out_first[...] = out[:rows]
    out_second[...] = out[rows:]


def run_shared(first, second, w_gate, w_up, w_down):
    rows, width = first.shape
    hidden = w_gate.shape[1]
    return pl.pallas_call(
        shared_kernel,
        out_shape=[jax.ShapeDtypeStruct((rows, width), BF16)] * 2,
        in_specs=[VMEM] * 5,
        out_specs=[VMEM] * 2,
        cost_estimate=pl.CostEstimate(
            flops=2 * 3 * 2 * rows * width * hidden,
            transcendentals=2 * rows * hidden,
            bytes_accessed=2 * (3 * width * hidden + 4 * rows * width),
        ),
        compiler_params=pltpu.CompilerParams(vmem_limit_bytes=48 << 20),
        name="shared_experts",
    )(first, second, w_gate, w_up, w_down)


def on_device(
    latents,
    expert_ids,
    gate_weights,
    capacity,
    hot_expert,
    w_gate,
    w_up,
    w_down,
    shared_gate,
    shared_up,
    shared_down,
):
    tokens, width = latents.shape
    half = tokens // 2
    experts = capacity.shape[1]
    local = w_gate.shape[0]
    count = lax.axis_size("expert")
    n_dp = lax.axis_size("dp")
    ring = ring_of(count)
    forward = [(ring[i], ring[(i + 1) % count]) for i in range(count)]
    backward = [(b, a) for a, b in forward]
    mid = count // 2

    own = [latents[:half], latents[half:]]
    blocks = {o: [None, None] for o in range(count)}
    for h in range(2):
        up, down = own[h], own[h]
        for hop in range(1, mid + 1):
            if hop < mid or h == 0:
                up = lax.ppermute(up, "expert", forward)
                blocks[hop][h] = up
            if hop < mid or h == 1:
                down = lax.ppermute(down, "expert", backward)
                blocks[count - hop][h] = down
    blocks[0] = [latents]

    info = routing(expert_ids, gate_weights, capacity, hot_expert, experts)
    meta = lax.all_to_all(
        info.reshape(count, 2 * local, tokens), "expert", split_axis=0, concat_axis=0, tiled=True
    )
    me = lax.axis_index("expert")
    table = []
    for e in range(count):
        at = ring.index(e)
        table.append([ring[(at - o) % count] for o in range(count)])
    idx = jnp.array(table, jnp.int32)[me]
    idx = jnp.concatenate([idx, (hot_expert - me * local).astype(jnp.int32)])

    bits = [1 << b for b in range(n_dp.bit_length() - 1)]
    near = {0: latents}
    for bit in reversed(bits):
        swap = [(d, d ^ bit) for d in range(n_dp)]
        for r in list(near):
            near[r ^ bit] = lax.ppermute(near[r], "dp", swap)
    part = {}
    for r in range(0, n_dp, 2):
        part[r], part[r + 1] = run_shared(near[r], near[r + 1], shared_gate, shared_up, shared_down)
    for bit in bits:
        swap = [(d, d ^ bit) for d in range(n_dp)]
        for r in sorted(part):
            if r & bit:
                came = lax.ppermute(part.pop(r), "dp", swap)
                total = part[r ^ bit].astype(F32) + came.astype(F32)
                part[r ^ bit] = total if len(bits) and bit == bits[-1] else total.astype(BF16)
    shared = part[0]

    weights = [jnp.swapaxes(w_gate, 1, 2), jnp.swapaxes(w_up, 1, 2), w_down]
    order = offsets_of(count)
    early, late = tuple(order[2:-2]), tuple(order[-2:] + order[:2])
    some = (local + 1) // 2
    groups = [g for g in (tuple(range(some)), tuple(range(some, local))) if g]
    held, chain = [], None
    for i, group in enumerate(groups):
        last = i == len(groups) - 1
        got = list(
            run_experts(early, [group], idx, meta, blocks, [weights], fetch=True, before=chain, final=last)
        )
        held.append(got[-3:])
        chain = flat = got[:-3]
    flat = flat + list(run_experts(late, groups, idx, meta, blocks, held))
    done = {}
    for i, o in enumerate(early + late):
        done[o] = [flat[2 * i], flat[2 * i + 1]]

    result = []
    for h in range(2):
        pieces = [done[0][h]]
        for step, perm, long in ((-1, forward, h == 0), (1, backward, h == 1)):
            start = mid if long else mid - 1
            acc = done[(step * start) % count][h]
            for k in range(start, 0, -1):
                came = lax.ppermute(acc, "expert", perm)
                if k > 1:
                    acc = (came.astype(F32) + done[(step * (k - 1)) % count][h].astype(F32)).astype(BF16)
            pieces.append(came)
        total = shared[h * half : (h + 1) * half].astype(F32)
        for piece in pieces:
            total = total + piece.astype(F32)
        result.append(total.astype(BF16))
    return jnp.concatenate(result, axis=0)


def solution(mesh):
    placed = (
        P(("dp", "expert"), None),
        P(("dp", "expert"), None),
        P(("dp", "expert"), None),
        P("dp", None),
        P("dp"),
        P("expert", None, None),
        P("expert", None, None),
        P("expert", None, None),
        P(None, "dp"),
        P(None, "dp"),
        P("dp", None),
    )
    return jax.shard_map(
        on_device, mesh=mesh, in_specs=placed, out_specs=P(("dp", "expert"), None), check_vma=False
    )
```

```python
import functools

import jax
import jax.numpy as jnp
from jax import lax
from jax.experimental import pallas as pl
from jax.experimental.pallas import tpu as pltpu
from jax.sharding import PartitionSpec as P

HOT_SLOTS = 40
SLOTS = 24
EXTRA = HOT_SLOTS - SLOTS
BF16 = jnp.bfloat16
F32 = jnp.float32
HBM = pl.BlockSpec(memory_space=pltpu.HBM)
VMEM = pl.BlockSpec(memory_space=pltpu.VMEM)
SMEM = pl.BlockSpec(memory_space=pltpu.SMEM)


def ring_of(count):
    return list(range(0, count, 2)) + list(range(count - 1, 0, -2))


def offsets_of(count):
    order = [0, count // 2]
    for hop in range(1, count // 2):
        order += [hop, count - hop]
    return order


def dot(a, b):
    return jnp.dot(a, b, preferred_element_type=F32)


def dot_t(a, b):
    return lax.dot_general(a, b, (((1,), (1,)), ((), ())), preferred_element_type=F32)


def dot_l(a, b):
    return lax.dot_general(a, b, (((0,), (0,)), ((), ())), preferred_element_type=F32)


def routing(expert_ids, gate_weights, capacity, hot_expert, experts):
    tokens, top = expert_ids.shape
    ids, gates = expert_ids.T, gate_weights.T
    labels = jnp.arange(experts, dtype=jnp.int32)[:, None]
    chosen = jnp.zeros((experts, tokens), jnp.bool_)
    weight = jnp.zeros((experts, tokens), F32)
    for k in range(top):
        here = ids[k][None, :] == labels
        chosen = chosen | here
        weight = weight + jnp.where(here, gates[k][None, :], 0.0)
    place = jnp.arange(tokens, dtype=jnp.int32)
    earlier = (place[:, None] < place[None, :]).astype(BF16)
    rank = dot(chosen.astype(BF16), earlier)
    limit = jnp.where(labels == hot_expert[0], HOT_SLOTS, capacity[0][:, None]).astype(F32)
    kept = chosen & (rank < limit)
    return jnp.stack([jnp.where(kept, rank, -1.0), jnp.where(kept, weight, 0.0)], axis=1)


def experts_kernel(offsets, sizes, local, buffers, idx, meta, *refs):
    refs = list(refs)
    units = [[refs.pop(0) for _ in range(size)] for size in sizes]
    source = [refs.pop(0) for _ in range(3)]
    outs = [[refs.pop(0) for _ in range(2)] for _ in offsets]
    held = [refs.pop(0) for _ in range(3)]
    sel, eo, rows, scale, sem = refs
    pairs = len(offsets) // 2
    width = rows.shape[2]
    wide, wide_x = 2 * SLOTS, 2 * EXTRA
    base = pairs * wide
    full = pairs * (wide + wide_x)
    hot = idx[idx.shape[0] - 1]

    def fetching(e, k):
        at = lax.rem(e, buffers)
        return pltpu.make_async_copy(source[k].at[e], held[k].at[at], sem.at[at, k])

    for e in range(min(buffers, local)):
        for k in range(3):
            fetching(e, k).start()

    lane = lax.broadcasted_iota(jnp.int32, (1, 256), 1)
    second = (lane >= 128).astype(F32)
    for p in range(pairs):
        info = [meta[idx[offsets[2 * p + i]]] for i in range(2)]
        blocks = []
        for e in range(local):
            rank = jnp.concatenate([info[0][2 * e : 2 * e + 1], info[1][2 * e : 2 * e + 1]], axis=1)
            gate = jnp.concatenate([info[0][2 * e + 1 : 2 * e + 2], info[1][2 * e + 1 : 2 * e + 2]], axis=1)
            key = jnp.where((rank >= 0) & (rank < SLOTS), rank + SLOTS * second, -1.0).astype(jnp.int32)
            pick = (lax.broadcasted_iota(jnp.int32, (wide, 256), 0) == key).astype(F32)
            blocks.append(pick)
            scale[e, pl.ds(p * wide, wide), :] = jnp.broadcast_to(
                jnp.sum(pick * gate, axis=1, keepdims=True), (wide, 128)
            )
            key_x = jnp.where((rank >= SLOTS) & (hot == e), rank - SLOTS + EXTRA * second, -1.0)
            pick_x = (lax.broadcasted_iota(jnp.int32, (wide_x, 256), 0) == key_x.astype(jnp.int32)).astype(F32)
            scale[e, pl.ds(base + p * wide_x, wide_x), :] = jnp.broadcast_to(
                jnp.sum(pick_x * gate, axis=1, keepdims=True), (wide_x, 128)
            )
            extra = pick_x if e == 0 else extra + pick_x
        blocks.append(extra)
        pick = jnp.concatenate(blocks, axis=0).astype(BF16)
        sel[p] = pick
        pair = jnp.concatenate([unit[...] for mine in units[2 * p : 2 * p + 2] for unit in mine], axis=0)
        got = dot(pick, pair).astype(BF16)
        for e in range(local):
            rows[e, pl.ds(p * wide, wide), :] = got[e * wide : (e + 1) * wide]

            @pl.when(hot == e)
            def _():
                rows[e, pl.ds(base + p * wide_x, wide_x), :] = got[local * wide :]

        eo[p, pl.ds(local * wide, wide_x), :] = jnp.zeros((wide_x, width), BF16)

    def run(e, length):
        at = lax.rem(e, buffers)
        tokens = rows[e, :length]
        gate = dot_t(tokens, held[0][at])
        upper = dot_t(tokens, held[1][at])
        hidden = (gate / (1.0 + jnp.exp(-gate)) * upper * scale[e, :length][:, :1]).astype(BF16)
        fetching(e, 2).wait()
        out = dot(hidden, held[2][at]).astype(BF16)
        for p in range(pairs):
            eo[p, pl.ds(pl.multiple_of(e * wide, wide), wide), :] = out[p * wide : (p + 1) * wide]
            if length > base:
                eo[p, pl.ds(local * wide, wide_x), :] = out[base + p * wide_x : base + (p + 1) * wide_x]

    def body(e, carry):
        fetching(e, 0).wait()
        fetching(e, 1).wait()

        @pl.when(hot == e)
        def _():
            run(e, full)

        @pl.when(hot != e)
        def _():
            run(e, base)

        @pl.when(e + buffers < local)
        def _():
            for k in range(3):
                fetching(e + buffers, k).start()

        return carry

    lax.fori_loop(0, local, body, 0)

    for p in range(pairs):
        total = dot_l(sel[p], eo[p]).astype(BF16)
        for i in range(4):
            outs[2 * p + i // 2][i % 2][...] = total[i * 64 : (i + 1) * 64]


def run_experts(offsets, local, idx, meta, blocks, weights):
    hidden, width = weights[2].shape[1:]
    wide, wide_x = 2 * SLOTS, 2 * EXTRA
    pairs = len(offsets) // 2
    high = local * wide + wide_x
    full = pairs * (wide + wide_x)
    buffers = min(local, 3)
    flat = [unit for o in offsets for unit in blocks[o]]
    sizes = tuple(len(blocks[o]) for o in offsets)
    room = 3 * buffers * hidden * width * 2 + local * full * (2 * width + 512) + pairs * high * (2 * width + 512)
    room += full * (6 * width + 10 * hidden) + (2 << 20)
    flat = [pltpu.with_memory_space_constraint(unit, pltpu.VMEM) for unit in flat]
    weights = [pltpu.with_memory_space_constraint(w, pltpu.HBM) for w in weights]
    flops = 2 * 3 * width * hidden * local * pairs * wide + 4 * len(offsets) * 128 * high * width
    return pl.pallas_call(
        functools.partial(experts_kernel, offsets, sizes, local, buffers),
        out_shape=[pltpu.VMEM((64, width), BF16)] * (2 * len(offsets)),
        in_specs=[SMEM, VMEM] + [VMEM] * len(flat) + [HBM] * 3,
        out_specs=[VMEM] * (2 * len(offsets)),
        scratch_shapes=[
            pltpu.VMEM((buffers, hidden, width), BF16),
            pltpu.VMEM((buffers, hidden, width), BF16),
            pltpu.VMEM((buffers, hidden, width), BF16),
            pltpu.VMEM((pairs, high, 256), BF16),
            pltpu.VMEM((pairs, high, width), BF16),
            pltpu.VMEM((local, full, width), BF16),
            pltpu.VMEM((local, full, 128), F32),
            pltpu.SemaphoreType.DMA((buffers, 3)),
        ],
        cost_estimate=pl.CostEstimate(
            flops=flops,
            transcendentals=local * pairs * wide * hidden,
            bytes_accessed=6 * local * hidden * width,
        ),
        compiler_params=pltpu.CompilerParams(vmem_limit_bytes=room),
        name="routed_experts",
    )(idx, meta, *flat, *weights)


def shared_kernel(first, second, w_gate, w_up, w_down, out_first, out_second):
    tokens = jnp.concatenate([first[...], second[...]], axis=0)
    gate = dot(tokens, w_gate[...])
    upper = dot(tokens, w_up[...])
    hidden = (gate / (1.0 + jnp.exp(-gate)) * upper).astype(BF16)
    out = dot(hidden, w_down[...]).astype(BF16)
    rows = first.shape[0]
    out_first[...] = out[:rows]
    out_second[...] = out[rows:]


def run_shared(first, second, w_gate, w_up, w_down):
    rows, width = first.shape
    hidden = w_gate.shape[1]
    return pl.pallas_call(
        shared_kernel,
        out_shape=[jax.ShapeDtypeStruct((rows, width), BF16)] * 2,
        in_specs=[VMEM] * 5,
        out_specs=[VMEM] * 2,
        cost_estimate=pl.CostEstimate(
            flops=2 * 3 * 2 * rows * width * hidden,
            transcendentals=2 * rows * hidden,
            bytes_accessed=2 * (3 * width * hidden + 4 * rows * width),
        ),
        compiler_params=pltpu.CompilerParams(vmem_limit_bytes=16 << 20),
        name="shared_experts",
    )(first, second, w_gate, w_up, w_down)


def on_device(
    latents,
    expert_ids,
    gate_weights,
    capacity,
    hot_expert,
    w_gate,
    w_up,
    w_down,
    shared_gate,
    shared_up,
    shared_down,
):
    tokens, width = latents.shape
    half = tokens // 2
    experts = capacity.shape[1]
    local = w_gate.shape[0]
    count = lax.axis_size("expert")
    n_dp = lax.axis_size("dp")
    ring = ring_of(count)
    forward = [(ring[i], ring[(i + 1) % count]) for i in range(count)]
    backward = [(b, a) for a, b in forward]
    mid = count // 2

    own = [latents[:half], latents[half:]]
    blocks = {o: [None, None] for o in range(count)}
    for h in range(2):
        up, down = own[h], own[h]
        for hop in range(1, mid + 1):
            if hop < mid or h == 0:
                up = lax.ppermute(up, "expert", forward)
                blocks[hop][h] = up
            if hop < mid or h == 1:
                down = lax.ppermute(down, "expert", backward)
                blocks[count - hop][h] = down
    blocks[0] = [latents]

    info = routing(expert_ids, gate_weights, capacity, hot_expert, experts)
    meta = lax.all_to_all(
        info.reshape(count, 2 * local, tokens), "expert", split_axis=0, concat_axis=0, tiled=True
    )
    me = lax.axis_index("expert")
    table = []
    for e in range(count):
        at = ring.index(e)
        table.append([ring[(at - o) % count] for o in range(count)])
    idx = jnp.array(table, jnp.int32)[me]
    idx = jnp.concatenate([idx, (hot_expert - me * local).astype(jnp.int32)])

    bits = [1 << b for b in range(n_dp.bit_length() - 1)]
    near = {0: latents}
    for bit in reversed(bits):
        swap = [(d, d ^ bit) for d in range(n_dp)]
        for r in list(near):
            near[r ^ bit] = lax.ppermute(near[r], "dp", swap)
    part = {}
    for r in range(0, n_dp, 2):
        part[r], part[r + 1] = run_shared(near[r], near[r + 1], shared_gate, shared_up, shared_down)
    weights = [jnp.swapaxes(w_gate, 1, 2), jnp.swapaxes(w_up, 1, 2), w_down]
    order = offsets_of(count)
    idx, *kept = lax.optimization_barrier((idx, *part.values()))
    part = dict(zip(part, kept))
    done = {}
    for at in range(0, count, 8):
        chunk = tuple(order[at : at + 8])
        flat = run_experts(chunk, local, idx, meta, blocks, weights)
        for i, o in enumerate(chunk):
            done[o] = [flat[2 * i], flat[2 * i + 1]]

    for bit in bits:
        swap = [(d, d ^ bit) for d in range(n_dp)]
        for r in sorted(part):
            if r & bit:
                came = lax.ppermute(part.pop(r), "dp", swap)
                total = part[r ^ bit].astype(F32) + came.astype(F32)
                part[r ^ bit] = total if bit == bits[-1] else total.astype(BF16)
    shared = part[0]

    result = []
    for h in range(2):
        pieces = [done[0][h]]
        for step, perm, long in ((-1, forward, h == 0), (1, backward, h == 1)):
            start = mid if long else mid - 1
            acc = done[(step * start) % count][h]
            for k in range(start, 0, -1):
                came = lax.ppermute(acc, "expert", perm)
                if k > 1:
                    acc = (came.astype(F32) + done[(step * (k - 1)) % count][h].astype(F32)).astype(BF16)
            pieces.append(came)
        total = shared[h * half : (h + 1) * half].astype(F32)
        for piece in pieces:
            total = total + piece.astype(F32)
        result.append(total.astype(BF16))
    return jnp.concatenate(result, axis=0)


def solution(mesh):
    placed = (
        P(("dp", "expert"), None),
        P(("dp", "expert"), None),
        P(("dp", "expert"), None),
        P("dp", None),
        P("dp"),
        P("expert", None, None),
        P("expert", None, None),
        P("expert", None, None),
        P(None, "dp"),
        P(None, "dp"),
        P("dp", None),
    )
    return jax.shard_map(
        on_device, mesh=mesh, in_specs=placed, out_specs=P(("dp", "expert"), None), check_vma=False
    )
```

```python
import functools

import jax
import jax.numpy as jnp
from jax import lax
from jax.experimental import pallas as pl
from jax.experimental.pallas import tpu as pltpu
from jax.sharding import PartitionSpec as P

HOT_SLOTS = 40
SLOTS = 24
SHARED_COST = 1000
EXTRA = HOT_SLOTS - SLOTS
BF16 = jnp.bfloat16
F32 = jnp.float32
HBM = pl.BlockSpec(memory_space=pltpu.HBM)
VMEM = pl.BlockSpec(memory_space=pltpu.VMEM)
SMEM = pl.BlockSpec(memory_space=pltpu.SMEM)


def ring_of(count):
    return list(range(0, count, 2)) + list(range(count - 1, 0, -2))


def offsets_of(count):
    order = [0, count // 2]
    for hop in range(1, count // 2):
        order += [hop, count - hop]
    return order


def dot(a, b):
    return jnp.dot(a, b, preferred_element_type=F32)


def dot_t(a, b):
    return lax.dot_general(a, b, (((1,), (1,)), ((), ())), preferred_element_type=F32)


def dot_l(a, b):
    return lax.dot_general(a, b, (((0,), (0,)), ((), ())), preferred_element_type=F32)


def routing(expert_ids, gate_weights, capacity, hot_expert, experts):
    tokens, top = expert_ids.shape
    ids, gates = expert_ids.T, gate_weights.T
    labels = jnp.arange(experts, dtype=jnp.int32)[:, None]
    chosen = jnp.zeros((experts, tokens), jnp.bool_)
    weight = jnp.zeros((experts, tokens), F32)
    for k in range(top):
        here = ids[k][None, :] == labels
        chosen = chosen | here
        weight = weight + jnp.where(here, gates[k][None, :], 0.0)
    place = jnp.arange(tokens, dtype=jnp.int32)
    earlier = (place[:, None] < place[None, :]).astype(BF16)
    rank = dot(chosen.astype(BF16), earlier)
    limit = jnp.where(labels == hot_expert[0], HOT_SLOTS, capacity[0][:, None]).astype(F32)
    kept = chosen & (rank < limit)
    return jnp.stack([jnp.where(kept, rank, -1.0), jnp.where(kept, weight, 0.0)], axis=1)


def experts_kernel(offsets, sizes, local, buffers, idx, meta, *refs):
    refs = list(refs)
    units = [[refs.pop(0) for _ in range(size)] for size in sizes]
    source = [refs.pop(0) for _ in range(3)]
    outs = [[refs.pop(0) for _ in range(2)] for _ in offsets]
    held = [refs.pop(0) for _ in range(3)]
    sel, eo, rows, scale, sem = refs
    pairs = len(offsets) // 2
    width = rows.shape[2]
    wide, wide_x = 2 * SLOTS, 2 * EXTRA
    base = pairs * wide
    full = pairs * (wide + wide_x)
    hot = idx[idx.shape[0] - 1]

    def fetching(e, k):
        at = lax.rem(e, buffers)
        return pltpu.make_async_copy(source[k].at[e], held[k].at[at], sem.at[at, k])

    for e in range(min(buffers, local)):
        for k in range(3):
            fetching(e, k).start()

    lane = lax.broadcasted_iota(jnp.int32, (1, 256), 1)
    second = (lane >= 128).astype(F32)
    for p in range(pairs):
        info = [meta[idx[offsets[2 * p + i]]] for i in range(2)]
        blocks = []
        for e in range(local):
            rank = jnp.concatenate([info[0][2 * e : 2 * e + 1], info[1][2 * e : 2 * e + 1]], axis=1)
            gate = jnp.concatenate([info[0][2 * e + 1 : 2 * e + 2], info[1][2 * e + 1 : 2 * e + 2]], axis=1)
            key = jnp.where((rank >= 0) & (rank < SLOTS), rank + SLOTS * second, -1.0).astype(jnp.int32)
            pick = (lax.broadcasted_iota(jnp.int32, (wide, 256), 0) == key).astype(F32)
            blocks.append(pick)
            scale[e, pl.ds(p * wide, wide), :] = jnp.broadcast_to(
                jnp.sum(pick * gate, axis=1, keepdims=True), (wide, 128)
            )
            key_x = jnp.where((rank >= SLOTS) & (hot == e), rank - SLOTS + EXTRA * second, -1.0)
            pick_x = (lax.broadcasted_iota(jnp.int32, (wide_x, 256), 0) == key_x.astype(jnp.int32)).astype(F32)
            scale[e, pl.ds(base + p * wide_x, wide_x), :] = jnp.broadcast_to(
                jnp.sum(pick_x * gate, axis=1, keepdims=True), (wide_x, 128)
            )
            extra = pick_x if e == 0 else extra + pick_x
        blocks.append(extra)
        pick = jnp.concatenate(blocks, axis=0).astype(BF16)
        sel[p] = pick
        pair = jnp.concatenate([unit[...] for mine in units[2 * p : 2 * p + 2] for unit in mine], axis=0)
        got = dot(pick, pair).astype(BF16)
        for e in range(local):
            rows[e, pl.ds(p * wide, wide), :] = got[e * wide : (e + 1) * wide]

            @pl.when(hot == e)
            def _():
                rows[e, pl.ds(base + p * wide_x, wide_x), :] = got[local * wide :]

        eo[p, pl.ds(local * wide, wide_x), :] = jnp.zeros((wide_x, width), BF16)

    def run(e, length):
        at = lax.rem(e, buffers)
        tokens = rows[e, :length]
        gate = dot_t(tokens, held[0][at])
        upper = dot_t(tokens, held[1][at])
        hidden = (gate / (1.0 + jnp.exp(-gate)) * upper * scale[e, :length][:, :1]).astype(BF16)
        fetching(e, 2).wait()
        out = dot(hidden, held[2][at]).astype(BF16)
        for p in range(pairs):
            eo[p, pl.ds(pl.multiple_of(e * wide, wide), wide), :] = out[p * wide : (p + 1) * wide]
            if length > base:
                eo[p, pl.ds(local * wide, wide_x), :] = out[base + p * wide_x : base + (p + 1) * wide_x]

    def body(e, carry):
        fetching(e, 0).wait()
        fetching(e, 1).wait()

        @pl.when(hot == e)
        def _():
            run(e, full)

        @pl.when(hot != e)
        def _():
            run(e, base)

        @pl.when(e + buffers < local)
        def _():
            for k in range(3):
                fetching(e + buffers, k).start()

        return carry

    lax.fori_loop(0, local, body, 0)

    for p in range(pairs):
        total = dot_l(sel[p], eo[p]).astype(BF16)
        for i in range(4):
            outs[2 * p + i // 2][i % 2][...] = total[i * 64 : (i + 1) * 64]


def run_experts(offsets, local, idx, meta, blocks, weights):
    hidden, width = weights[2].shape[1:]
    wide, wide_x = 2 * SLOTS, 2 * EXTRA
    pairs = len(offsets) // 2
    high = local * wide + wide_x
    full = pairs * (wide + wide_x)
    buffers = min(local, 3)
    flat = [unit for o in offsets for unit in blocks[o]]
    sizes = tuple(len(blocks[o]) for o in offsets)
    room = 3 * buffers * hidden * width * 2 + local * full * (2 * width + 512) + pairs * high * (2 * width + 512)
    room += full * (6 * width + 10 * hidden) + (2 << 20)
    flat = [pltpu.with_memory_space_constraint(unit, pltpu.VMEM) for unit in flat]
    weights = [pltpu.with_memory_space_constraint(w, pltpu.HBM) for w in weights]
    flops = 2 * 3 * width * hidden * local * pairs * wide + 4 * len(offsets) * 128 * high * width
    return pl.pallas_call(
        functools.partial(experts_kernel, offsets, sizes, local, buffers),
        out_shape=[pltpu.VMEM((64, width), BF16)] * (2 * len(offsets)),
        in_specs=[SMEM, VMEM] + [VMEM] * len(flat) + [HBM] * 3,
        out_specs=[VMEM] * (2 * len(offsets)),
        scratch_shapes=[
            pltpu.VMEM((buffers, hidden, width), BF16),
            pltpu.VMEM((buffers, hidden, width), BF16),
            pltpu.VMEM((buffers, hidden, width), BF16),
            pltpu.VMEM((pairs, high, 256), BF16),
            pltpu.VMEM((pairs, high, width), BF16),
            pltpu.VMEM((local, full, width), BF16),
            pltpu.VMEM((local, full, 128), F32),
            pltpu.SemaphoreType.DMA((buffers, 3)),
        ],
        cost_estimate=pl.CostEstimate(
            flops=flops,
            transcendentals=local * pairs * wide * hidden,
            bytes_accessed=6 * local * hidden * width,
        ),
        compiler_params=pltpu.CompilerParams(vmem_limit_bytes=room),
        name="routed_experts",
    )(idx, meta, *flat, *weights)


def shared_kernel(count, *refs):
    blocks, weights, outs = refs[:count], refs[count : count + 3], refs[count + 3 : count + 5]
    x, wg, wu, wd, out, sem = refs[count + 5 :]
    rows = blocks[0].shape[0]
    loads = [
        pltpu.make_async_copy(block, x.at[pl.ds(i * rows, rows)], sem.at[i]) for i, block in enumerate(blocks)
    ]
    loads += [
        pltpu.make_async_copy(source, target, sem.at[count + k])
        for k, (source, target) in enumerate(zip(weights, (wg, wu, wd)))
    ]
    for copy in loads:
        copy.start()
    for copy in loads[:-2]:
        copy.wait()
    gate = dot(x[...], wg[...])
    loads[-2].wait()
    upper = dot(x[...], wu[...])
    hidden = (gate / (1.0 + jnp.exp(-gate)) * upper).astype(BF16)
    loads[-1].wait()
    half = count * rows // 2
    stores = []
    for i in (1, 0):
        out[i] = dot(hidden[i * half : (i + 1) * half], wd[...]).astype(BF16)
        stores.append(pltpu.make_async_copy(out.at[i], outs[i], sem.at[count + 3 + i]))
        stores[-1].start()
    for copy in stores:
        copy.wait()


def run_shared(blocks, weights):
    count = len(blocks)
    rows, width = blocks[0].shape
    hidden = weights[0].shape[1]
    blocks = [pltpu.with_memory_space_constraint(block, pltpu.HBM) for block in blocks]
    weights = [pltpu.with_memory_space_constraint(w, pltpu.HBM) for w in weights]
    return pl.pallas_call(
        functools.partial(shared_kernel, count),
        out_shape=[pltpu.HBM((count * rows // 2, width), BF16)] * 2,
        in_specs=[HBM] * (count + 3),
        out_specs=[HBM] * 2,
        scratch_shapes=[
            pltpu.VMEM((count * rows, width), BF16),
            pltpu.VMEM((width, hidden), BF16),
            pltpu.VMEM((width, hidden), BF16),
            pltpu.VMEM((hidden, width), BF16),
            pltpu.VMEM((2, count * rows // 2, width), BF16),
            pltpu.SemaphoreType.DMA((count + 5,)),
        ],
        cost_estimate=pl.CostEstimate(
            flops=SHARED_COST, transcendentals=0, bytes_accessed=SHARED_COST,
        ),
        compiler_params=pltpu.CompilerParams(vmem_limit_bytes=26 << 20),
        name="shared_experts",
    )(*blocks, *weights)


def tied(values, anchors):
    return lax.optimization_barrier((tuple(values), tuple(anchors)))[0]


def on_device(
    latents,
    expert_ids,
    gate_weights,
    capacity,
    hot_expert,
    w_gate,
    w_up,
    w_down,
    shared_gate,
    shared_up,
    shared_down,
):
    tokens, width = latents.shape
    half = tokens // 2
    experts = capacity.shape[1]
    local = w_gate.shape[0]
    count = lax.axis_size("expert")
    n_dp = lax.axis_size("dp")
    ring = ring_of(count)
    forward = [(ring[i], ring[(i + 1) % count]) for i in range(count)]
    backward = [(b, a) for a, b in forward]
    mid = count // 2

    info = routing(expert_ids, gate_weights, capacity, hot_expert, experts)
    meta = lax.all_to_all(
        info.reshape(count, 2 * local, tokens), "expert", split_axis=0, concat_axis=0, tiled=True
    )
    me = lax.axis_index("expert")
    table = []
    for e in range(count):
        at = ring.index(e)
        table.append([ring[(at - o) % count] for o in range(count)])
    idx = jnp.array(table, jnp.int32)[me]
    idx = jnp.concatenate([idx, (hot_expert - me * local).astype(jnp.int32)])

    bits = [1 << b for b in range(n_dp.bit_length() - 1)]
    blocks = {o: [None, None] for o in range(count)}
    up, down = [latents[:half], latents[half:]], [latents[:half], latents[half:]]
    for hop in range(1, mid + 1):
        for h in range(2):
            if hop < mid or h == 0:
                up[h] = lax.ppermute(up[h], "expert", forward)
                blocks[hop][h] = up[h]
            if hop < mid or h == 1:
                down[h] = lax.ppermute(down[h], "expert", backward)
                blocks[count - hop][h] = down[h]
    blocks[0] = [latents]
    mine = [latents]
    for bit in reversed(bits[1:]):
        swap = [(d, d ^ bit) for d in range(n_dp)]
        mine += [lax.ppermute(block, "dp", swap) for block in mine]
    mine = jnp.concatenate(mine, axis=0)
    swap = [(d, d ^ 1) for d in range(n_dp)]
    keep, give = run_shared([mine, lax.ppermute(mine, "dp", swap)], (shared_gate, shared_up, shared_down))
    (idx,), (keep, give) = lax.optimization_barrier(((idx,), (keep, give)))
    shared = keep.astype(F32) + lax.ppermute(give, "dp", swap).astype(F32)
    where = [0]
    for bit in reversed(bits[1:]):
        where += [r ^ bit for r in where]
    part = {r: shared[i * tokens : (i + 1) * tokens] for i, r in enumerate(where)}
    for bit in bits[1:]:
        swap = [(d, d ^ bit) for d in range(n_dp)]
        for r in sorted(part):
            if r & bit:
                came = lax.ppermute(part.pop(r).astype(BF16), "dp", swap)
                part[r ^ bit] = part[r ^ bit] + came.astype(F32)
    shared = part[0]

    weights = [jnp.swapaxes(w_gate, 1, 2), jnp.swapaxes(w_up, 1, 2), w_down]
    order = offsets_of(count)
    done = {}
    for at in range(0, count, 8):
        chunk = tuple(order[at : at + 8])
        flat = run_experts(chunk, local, idx, meta, blocks, weights)
        for i, o in enumerate(chunk):
            done[o] = [flat[2 * i], flat[2 * i + 1]]

    result = []
    for h in range(2):
        pieces = [done[0][h]]
        for step, perm, long in ((-1, forward, h == 0), (1, backward, h == 1)):
            start = mid if long else mid - 1
            acc = done[(step * start) % count][h]
            for k in range(start, 0, -1):
                came = lax.ppermute(acc, "expert", perm)
                if k > 1:
                    acc = (came.astype(F32) + done[(step * (k - 1)) % count][h].astype(F32)).astype(BF16)
            pieces.append(came)
        total = shared[h * half : (h + 1) * half].astype(F32)
        for piece in pieces:
            total = total + piece.astype(F32)
        result.append(total.astype(BF16))
    return jnp.concatenate(result, axis=0)


def solution(mesh):
    placed = (
        P(("dp", "expert"), None),
        P(("dp", "expert"), None),
        P(("dp", "expert"), None),
        P("dp", None),
        P("dp"),
        P("expert", None, None),
        P("expert", None, None),
        P("expert", None, None),
        P(None, "dp"),
        P(None, "dp"),
        P("dp", None),
    )
    return jax.shard_map(
        on_device, mesh=mesh, in_specs=placed, out_specs=P(("dp", "expert"), None), check_vma=False
    )
```

```python
import functools

import jax
import jax.numpy as jnp
from jax import lax
from jax.experimental import pallas as pl
from jax.experimental.pallas import tpu as pltpu
from jax.sharding import PartitionSpec as P

HOT_SLOTS = 40
SLOTS = 24
SMALL = 1000
EXTRA = HOT_SLOTS - SLOTS
BF16 = jnp.bfloat16
F32 = jnp.float32
HBM = pl.BlockSpec(memory_space=pltpu.HBM)
VMEM = pl.BlockSpec(memory_space=pltpu.VMEM)
SMEM = pl.BlockSpec(memory_space=pltpu.SMEM)


def ring_of(count):
    return list(range(0, count, 2)) + list(range(count - 1, 0, -2))


def offsets_of(count):
    order = [0, count // 2]
    for hop in range(1, count // 2):
        order += [hop, count - hop]
    return order


def dot(a, b):
    return jnp.dot(a, b, preferred_element_type=F32)


def dot_t(a, b):
    return lax.dot_general(a, b, (((1,), (1,)), ((), ())), preferred_element_type=F32)


def dot_l(a, b):
    return lax.dot_general(a, b, (((0,), (0,)), ((), ())), preferred_element_type=F32)


def routing(expert_ids, gate_weights, capacity, hot_expert, experts):
    tokens, top = expert_ids.shape
    ids, gates = expert_ids.T, gate_weights.T
    labels = jnp.arange(experts, dtype=jnp.int32)[:, None]
    chosen = jnp.zeros((experts, tokens), jnp.bool_)
    weight = jnp.zeros((experts, tokens), F32)
    for k in range(top):
        here = ids[k][None, :] == labels
        chosen = chosen | here
        weight = weight + jnp.where(here, gates[k][None, :], 0.0)
    place = jnp.arange(tokens, dtype=jnp.int32)
    earlier = (place[:, None] < place[None, :]).astype(BF16)
    rank = dot(chosen.astype(BF16), earlier)
    limit = jnp.where(labels == hot_expert[0], HOT_SLOTS, capacity[0][:, None]).astype(F32)
    kept = chosen & (rank < limit)
    return jnp.stack([jnp.where(kept, rank, -1.0), jnp.where(kept, weight, 0.0)], axis=1)


def source_of(place, offset, count):
    at = jnp.where(place % 2 == 0, place // 2, count // 2 + (count - 1 - place) // 2)
    at = lax.rem(at - offset + count, count)
    return jnp.where(at < count // 2, 2 * at, 2 * count - 1 - 2 * at)


def pick_kernel(offsets, early, sizes, count, local, where, meta, *refs):
    refs = list(refs)
    units = [[refs.pop(0) for _ in range(size)] for size in sizes]
    sel, scale, rows = refs
    pairs = len(offsets) // 2
    wide, wide_x = 2 * SLOTS, 2 * EXTRA
    base, base_e = pairs * wide, early * wide
    hot = where[1]
    lane = lax.broadcasted_iota(jnp.int32, (1, 256), 1)
    second = (lane >= 128).astype(F32)
    for p in range(pairs):
        info = [meta[source_of(where[0], offsets[2 * p + i], count)] for i in range(2)]
        blocks = []
        for e in range(local):
            rank = jnp.concatenate([part[2 * e : 2 * e + 1] for part in info], axis=1)
            gate = jnp.concatenate([part[2 * e + 1 : 2 * e + 2] for part in info], axis=1)
            key = jnp.where((rank >= 0) & (rank < SLOTS), rank + SLOTS * second, -1.0).astype(jnp.int32)
            pick = (lax.broadcasted_iota(jnp.int32, (wide, 256), 0) == key).astype(F32)
            blocks.append(pick)
            scale[e, pl.ds(p * wide, wide), :] = jnp.broadcast_to(
                jnp.sum(pick * gate, axis=1, keepdims=True), (wide, 128)
            )
            key_x = jnp.where((rank >= SLOTS) & (hot == e), rank - SLOTS + EXTRA * second, -1.0)
            pick_x = (lax.broadcasted_iota(jnp.int32, (wide_x, 256), 0) == key_x.astype(jnp.int32)).astype(F32)
            scale[e, pl.ds(base + p * wide_x, wide_x), :] = jnp.broadcast_to(
                jnp.sum(pick_x * gate, axis=1, keepdims=True), (wide_x, 128)
            )
            extra = pick_x if e == 0 else extra + pick_x
        blocks.append(extra)
        sel[p] = jnp.concatenate(blocks, axis=0).astype(BF16)
        if p < early:
            gather_pair(sel[p], units[2 * p] + units[2 * p + 1], rows, p, base_e, local, hot)


def gather_pair(pick, units, rows, p, base, local, hot):
    wide, wide_x = 2 * SLOTS, 2 * EXTRA
    pair = jnp.concatenate([unit[...] for unit in units], axis=0)
    got = dot(pick, pair).astype(BF16)
    for e in range(local):
        rows[e, pl.ds(p * wide, wide), :] = got[e * wide : (e + 1) * wide]

        @pl.when(hot == e)
        def _():
            rows[e, pl.ds(base + p * wide_x, wide_x), :] = got[local * wide :]


def run_pick(offsets, early, count, local, where, meta, blocks):
    flat = [unit for o in offsets[: 2 * early] for unit in blocks[o]]
    sizes = tuple(len(blocks[o]) for o in offsets[: 2 * early])
    width = flat[0].shape[1]
    pairs = len(offsets) // 2
    wide, wide_x = 2 * SLOTS, 2 * EXTRA
    flat = [pltpu.with_memory_space_constraint(unit, pltpu.VMEM) for unit in flat]
    return pl.pallas_call(
        functools.partial(pick_kernel, offsets, early, sizes, count, local),
        out_shape=[
            pltpu.VMEM((pairs, local * wide + wide_x, 256), BF16),
            pltpu.VMEM((local, pairs * (wide + wide_x), 128), F32),
            pltpu.VMEM((local, early * (wide + wide_x), width), BF16),
        ],
        in_specs=[SMEM, VMEM] + [VMEM] * len(flat),
        out_specs=[VMEM] * 3,
        cost_estimate=pl.CostEstimate(flops=SMALL, transcendentals=0, bytes_accessed=SMALL),
        compiler_params=pltpu.CompilerParams(vmem_limit_bytes=6 << 20),
        name="pick",
    )(where, meta, *flat)


def experts_kernel(offsets, early, sizes, local, buffers, where, sel, scale, rows_e, *refs):
    refs = list(refs)
    units = [[refs.pop(0) for _ in range(size)] for size in sizes]
    ready = [refs.pop(0) for _ in range(3)]
    source = [refs.pop(0) for _ in range(3)]
    outs = [[refs.pop(0) for _ in range(2)] for _ in offsets]
    held = [refs.pop(0) for _ in range(3)]
    eo, rows, sem = refs
    pairs = len(offsets) // 2
    late = pairs - early
    width = rows.shape[2]
    wide, wide_x = 2 * SLOTS, 2 * EXTRA
    base, base_e, base_l = pairs * wide, early * wide, late * wide
    hot = where[1]

    def fetching(e, k):
        at = lax.rem(e - 1, buffers)
        return pltpu.make_async_copy(source[k].at[e], held[k].at[at], sem.at[at, k])

    for e in range(1, min(buffers + 1, local)):
        for k in range(3):
            fetching(e, k).start()

    for p in range(late):
        gather_pair(sel[early + p], units[2 * p] + units[2 * p + 1], rows, p, base_l, local, hot)
    for p in range(pairs):
        eo[p, pl.ds(local * wide, wide_x), :] = jnp.zeros((wide_x, width), BF16)

    def run(e, gates, uppers, downs, before_down, whole):
        tokens = [rows_e[e, :base_e], rows[e, :base_l]]
        if whole:
            tokens += [rows_e[e, base_e:], rows[e, base_l:]]
        tokens = jnp.concatenate(tokens, axis=0)
        gate = dot_t(tokens, gates[...])
        upper = dot_t(tokens, uppers[...])
        weight = scale[e, : tokens.shape[0]][:, :1]
        hidden = (gate / (1.0 + jnp.exp(-gate)) * upper * weight).astype(BF16)
        before_down()
        out = dot(hidden, downs[...]).astype(BF16)
        for p in range(pairs):
            at = e * wide if isinstance(e, int) else pl.multiple_of(e * wide, wide)
            eo[p, pl.ds(at, wide), :] = out[p * wide : (p + 1) * wide]
            if whole:
                eo[p, pl.ds(local * wide, wide_x), :] = out[base + p * wide_x : base + (p + 1) * wide_x]

    def either(e, *rest):
        @pl.when(hot == e)
        def _():
            run(e, *rest, True)

        @pl.when(hot != e)
        def _():
            run(e, *rest, False)

    either(0, *ready, lambda: None)

    def body(e, carry):
        at = lax.rem(e - 1, buffers)
        fetching(e, 0).wait()
        fetching(e, 1).wait()
        either(e, *(w.at[at] for w in held), lambda: fetching(e, 2).wait())

        @pl.when(e + buffers < local)
        def _():
            for k in range(3):
                fetching(e + buffers, k).start()

        return carry

    lax.fori_loop(1, local, body, 0)

    for p in range(pairs):
        total = dot_l(sel[p], eo[p]).astype(BF16)
        for i in range(4):
            outs[2 * p + i // 2][i % 2][...] = total[i * 64 : (i + 1) * 64]


def run_experts(offsets, early, local, where, picked, blocks, ready, weights):
    hidden, width = weights[2].shape[1:]
    wide, wide_x = 2 * SLOTS, 2 * EXTRA
    pairs = len(offsets) // 2
    late = pairs - early
    high = local * wide + wide_x
    full, full_l = pairs * (wide + wide_x), late * (wide + wide_x)
    buffers = max(1, min(local - 1, 2))
    flat = [unit for o in offsets[2 * early :] for unit in blocks[o]]
    sizes = tuple(len(blocks[o]) for o in offsets[2 * early :])
    room = 2 * width * (3 * buffers * hidden + local * full_l + pairs * high)
    room += full * (6 * width + 10 * hidden) + (2 << 20)
    inside = [pltpu.with_memory_space_constraint(v, pltpu.VMEM) for v in [*picked, *flat, *ready]]
    weights = [pltpu.with_memory_space_constraint(w, pltpu.HBM) for w in weights]
    return pl.pallas_call(
        functools.partial(experts_kernel, offsets, early, sizes, local, buffers),
        out_shape=[pltpu.VMEM((64, width), BF16)] * (2 * len(offsets)),
        in_specs=[SMEM] + [VMEM] * len(inside) + [HBM] * 3,
        out_specs=[VMEM] * (2 * len(offsets)),
        scratch_shapes=[
            pltpu.VMEM((buffers, hidden, width), BF16),
            pltpu.VMEM((buffers, hidden, width), BF16),
            pltpu.VMEM((buffers, hidden, width), BF16),
            pltpu.VMEM((pairs, high, width), BF16),
            pltpu.VMEM((local, full_l, width), BF16),
            pltpu.SemaphoreType.DMA((buffers, 3)),
        ],
        cost_estimate=pl.CostEstimate(
            flops=2 * 3 * width * hidden * local * pairs * wide + 4 * len(offsets) * 128 * high * width,
            transcendentals=local * pairs * wide * hidden,
            bytes_accessed=6 * local * hidden * width,
        ),
        compiler_params=pltpu.CompilerParams(vmem_limit_bytes=room),
        name="routed_experts",
    )(where, *inside, *weights)


def shared_kernel(count, *refs):
    blocks, weights, ahead = refs[:count], refs[count : count + 3], refs[count + 3 : count + 6]
    outs, ready = refs[count + 6 : count + 8], refs[count + 8 : count + 11]
    x, wg, wu, wd, out, sem, sem_r = refs[count + 11 :]
    rows = blocks[0].shape[0]
    loads = [
        pltpu.make_async_copy(block, x.at[pl.ds(i * rows, rows)], sem.at[i]) for i, block in enumerate(blocks)
    ]
    loads += [
        pltpu.make_async_copy(source, target, sem.at[count + k])
        for k, (source, target) in enumerate(zip(weights, (wg, wu, wd)))
    ]
    fetches = [
        pltpu.make_async_copy(source.at[0], target, sem_r.at[k])
        for k, (source, target) in enumerate(zip(ahead, ready))
    ]
    for copy in loads + fetches:
        copy.start()
    for copy in loads[:-2]:
        copy.wait()
    gate = dot(x[...], wg[...])
    loads[-2].wait()
    upper = dot(x[...], wu[...])
    hidden = (gate / (1.0 + jnp.exp(-gate)) * upper).astype(BF16)
    loads[-1].wait()
    half = count * rows // 2
    stores = []
    for i in (1, 0):
        out[i] = dot(hidden[i * half : (i + 1) * half], wd[...]).astype(BF16)
        stores.append(pltpu.make_async_copy(out.at[i], outs[i], sem.at[count + 3 + i]))
        stores[-1].start()
    for copy in fetches + stores:
        copy.wait()


def run_shared(blocks, weights, ahead):
    count = len(blocks)
    rows, width = blocks[0].shape
    hidden = weights[0].shape[1]
    blocks = [pltpu.with_memory_space_constraint(block, pltpu.HBM) for block in blocks]
    weights = [pltpu.with_memory_space_constraint(w, pltpu.HBM) for w in [*weights, *ahead]]
    return pl.pallas_call(
        functools.partial(shared_kernel, count),
        out_shape=[pltpu.HBM((count * rows // 2, width), BF16)] * 2
        + [pltpu.VMEM(w.shape[1:], BF16) for w in ahead],
        in_specs=[HBM] * (count + 6),
        out_specs=[HBM] * 2 + [VMEM] * 3,
        scratch_shapes=[
            pltpu.VMEM((count * rows, width), BF16),
            pltpu.VMEM((width, hidden), BF16),
            pltpu.VMEM((width, hidden), BF16),
            pltpu.VMEM((hidden, width), BF16),
            pltpu.VMEM((2, count * rows // 2, width), BF16),
            pltpu.SemaphoreType.DMA((count + 5,)),
            pltpu.SemaphoreType.DMA((3,)),
        ],
        cost_estimate=pl.CostEstimate(
            flops=SMALL, transcendentals=0, bytes_accessed=SMALL,
        ),
        compiler_params=pltpu.CompilerParams(vmem_limit_bytes=20 << 20),
        name="shared_experts",
    )(*blocks, *weights)


def tied(values, anchors):
    return lax.optimization_barrier((tuple(values), tuple(anchors)))[0]


def on_device(
    latents,
    expert_ids,
    gate_weights,
    capacity,
    hot_expert,
    w_gate,
    w_up,
    w_down,
    shared_gate,
    shared_up,
    shared_down,
):
    tokens, width = latents.shape
    half = tokens // 2
    local = w_gate.shape[0]
    count = lax.axis_size("expert")
    n_dp = lax.axis_size("dp")
    ring = ring_of(count)
    forward = [(ring[i], ring[(i + 1) % count]) for i in range(count)]
    backward = [(b, a) for a, b in forward]
    mid = count // 2

    info = routing(expert_ids, gate_weights, capacity, hot_expert, capacity.shape[1])
    info = info.reshape(count, 2 * local, tokens)
    meta = lax.all_to_all(info, "expert", split_axis=0, concat_axis=0, tiled=True)
    me = lax.axis_index("expert")
    where = jnp.stack([me, hot_expert[0] - me * local]).astype(jnp.int32)
    weights = [jnp.swapaxes(w_gate, 1, 2), jnp.swapaxes(w_up, 1, 2), w_down]

    bits = [1 << b for b in range(n_dp.bit_length() - 1)]
    blocks = {o: [None, None] for o in range(count)}
    up, down = [latents[:half], latents[half:]], [latents[:half], latents[half:]]
    for hop in range(1, mid + 1):
        if hop == mid:
            blocks[0] = [latents]
            order = offsets_of(count)
            order = order[2:-2] + order[-2:] + order[:2]
            picked = run_pick(tuple(order[:8]), 2, count, local, where, meta, blocks)
            up[0], down[1] = tied([up[0], down[1]], [picked[1]])
        for h in range(2):
            if hop < mid or h == 0:
                up[h] = lax.ppermute(up[h], "expert", forward)
                blocks[hop][h] = up[h]
            if hop < mid or h == 1:
                down[h] = lax.ppermute(down[h], "expert", backward)
                blocks[count - hop][h] = down[h]
    mine = [latents]
    for bit in reversed(bits[1:]):
        swap = [(d, d ^ bit) for d in range(n_dp)]
        mine += [lax.ppermute(block, "dp", swap) for block in mine]
    mine = jnp.concatenate(mine, axis=0)
    swap = [(d, d ^ 1) for d in range(n_dp)]
    keep, give, *ready = run_shared(
        [mine, lax.ppermute(mine, "dp", swap)], (shared_gate, shared_up, shared_down), weights
    )
    shared = keep.astype(F32) + lax.ppermute(give, "dp", swap).astype(F32)
    turns = [0]
    for bit in reversed(bits[1:]):
        turns += [r ^ bit for r in turns]
    part = {r: shared[i * tokens : (i + 1) * tokens] for i, r in enumerate(turns)}
    for bit in bits[1:]:
        swap = [(d, d ^ bit) for d in range(n_dp)]
        for r in sorted(part):
            if r & bit:
                came = lax.ppermute(part.pop(r).astype(BF16), "dp", swap)
                part[r ^ bit] = part[r ^ bit] + came.astype(F32)
    shared = part[0]

    done = {}
    for at in range(0, count, 8):
        chunk = tuple(order[at : at + 8])
        if at > 0:
            picked = run_pick(chunk, 2, count, local, where, meta, blocks)
        flat = run_experts(chunk, 2, local, where, picked, blocks, ready, weights)
        for i, o in enumerate(chunk):
            done[o] = [flat[2 * i], flat[2 * i + 1]]

    result = []
    for h in range(2):
        pieces = [done[0][h]]
        for step, perm, long in ((-1, forward, h == 0), (1, backward, h == 1)):
            start = mid if long else mid - 1
            acc = done[(step * start) % count][h]
            for k in range(start, 0, -1):
                came = lax.ppermute(acc, "expert", perm)
                if k > 1:
                    acc = (came.astype(F32) + done[(step * (k - 1)) % count][h].astype(F32)).astype(BF16)
            pieces.append(came)
        total = shared[h * half : (h + 1) * half].astype(F32)
        for piece in pieces:
            total = total + piece.astype(F32)
        result.append(total.astype(BF16))
    return jnp.concatenate(result, axis=0)


def solution(mesh):
    placed = (
        P(("dp", "expert"), None),
        P(("dp", "expert"), None),
        P(("dp", "expert"), None),
        P("dp", None),
        P("dp"),
        P("expert", None, None),
        P("expert", None, None),
        P("expert", None, None),
        P(None, "dp"),
        P(None, "dp"),
        P("dp", None),
    )
    return jax.shard_map(
        on_device, mesh=mesh, in_specs=placed, out_specs=P(("dp", "expert"), None), check_vma=False
    )
```

```python
import functools

import jax
import jax.numpy as jnp
from jax import lax
from jax.experimental import pallas as pl
from jax.experimental.pallas import tpu as pltpu
from jax.sharding import PartitionSpec as P

HOT_SLOTS = 40
SLOTS = 24
SMALL = 1000
EXTRA = HOT_SLOTS - SLOTS
BF16 = jnp.bfloat16
F32 = jnp.float32
HBM = pl.BlockSpec(memory_space=pltpu.HBM)
VMEM = pl.BlockSpec(memory_space=pltpu.VMEM)
SMEM = pl.BlockSpec(memory_space=pltpu.SMEM)


def ring_of(count):
    return list(range(0, count, 2)) + list(range(count - 1, 0, -2))


def offsets_of(count):
    order = [0, count // 2]
    for hop in range(1, count // 2):
        order += [hop, count - hop]
    return order


def dot(a, b):
    return jnp.dot(a, b, preferred_element_type=F32)


def dot_t(a, b):
    return lax.dot_general(a, b, (((1,), (1,)), ((), ())), preferred_element_type=F32)


def dot_l(a, b):
    return lax.dot_general(a, b, (((0,), (0,)), ((), ())), preferred_element_type=F32)


def routing(expert_ids, gate_weights, capacity, hot_expert, experts):
    tokens, top = expert_ids.shape
    ids, gates = expert_ids.T, gate_weights.T
    labels = jnp.arange(experts, dtype=jnp.int32)[:, None]
    chosen = jnp.zeros((experts, tokens), jnp.bool_)
    weight = jnp.zeros((experts, tokens), F32)
    for k in range(top):
        here = ids[k][None, :] == labels
        chosen = chosen | here
        weight = weight + jnp.where(here, gates[k][None, :], 0.0)
    place = jnp.arange(tokens, dtype=jnp.int32)
    earlier = (place[:, None] < place[None, :]).astype(BF16)
    rank = dot(chosen.astype(BF16), earlier)
    limit = jnp.where(labels == hot_expert[0], HOT_SLOTS, capacity[0][:, None]).astype(F32)
    kept = chosen & (rank < limit)
    return jnp.stack([jnp.where(kept, rank, -1.0), jnp.where(kept, weight, 0.0)], axis=1)


def source_of(place, offset, count):
    at = jnp.where(place % 2 == 0, place // 2, count // 2 + (count - 1 - place) // 2)
    at = lax.rem(at - offset + count, count)
    return jnp.where(at < count // 2, 2 * at, 2 * count - 1 - 2 * at)


def pick_kernel(offsets, early, sizes, count, local, where, meta, *refs):
    refs = list(refs)
    units = [[refs.pop(0) for _ in range(size)] for size in sizes]
    sel, scale, rows = refs
    pairs = len(offsets) // 2
    wide, wide_x = 2 * SLOTS, 2 * EXTRA
    base, base_e = pairs * wide, early * wide
    hot = where[1]
    lane = lax.broadcasted_iota(jnp.int32, (1, 256), 1)
    second = (lane >= 128).astype(F32)
    for p in range(pairs):
        info = [meta[source_of(where[0], offsets[2 * p + i], count)] for i in range(2)]
        blocks = []
        for e in range(local):
            rank = jnp.concatenate([part[2 * e : 2 * e + 1] for part in info], axis=1)
            gate = jnp.concatenate([part[2 * e + 1 : 2 * e + 2] for part in info], axis=1)
            key = jnp.where((rank >= 0) & (rank < SLOTS), rank + SLOTS * second, -1.0).astype(jnp.int32)
            pick = (lax.broadcasted_iota(jnp.int32, (wide, 256), 0) == key).astype(F32)
            blocks.append(pick)
            scale[e, pl.ds(p * wide, wide), :] = jnp.broadcast_to(
                jnp.sum(pick * gate, axis=1, keepdims=True), (wide, 128)
            )
            key_x = jnp.where((rank >= SLOTS) & (hot == e), rank - SLOTS + EXTRA * second, -1.0)
            pick_x = (lax.broadcasted_iota(jnp.int32, (wide_x, 256), 0) == key_x.astype(jnp.int32)).astype(F32)
            scale[e, pl.ds(base + p * wide_x, wide_x), :] = jnp.broadcast_to(
                jnp.sum(pick_x * gate, axis=1, keepdims=True), (wide_x, 128)
            )
            extra = pick_x if e == 0 else extra + pick_x
        blocks.append(extra)
        sel[p] = jnp.concatenate(blocks, axis=0).astype(BF16)
        if p < early:
            gather_pair(sel[p], units[2 * p] + units[2 * p + 1], rows, p, base_e, local, hot)


def gather_pair(pick, units, rows, p, base, local, hot):
    wide, wide_x = 2 * SLOTS, 2 * EXTRA
    pair = jnp.concatenate([unit[...] for unit in units], axis=0)
    got = dot(pick, pair).astype(BF16)
    for e in range(local):
        rows[e, pl.ds(p * wide, wide), :] = got[e * wide : (e + 1) * wide]

        @pl.when(hot == e)
        def _():
            rows[e, pl.ds(base + p * wide_x, wide_x), :] = got[local * wide :]


def run_pick(offsets, early, count, local, where, meta, blocks):
    flat = [unit for o in offsets[: 2 * early] for unit in blocks[o]]
    sizes = tuple(len(blocks[o]) for o in offsets[: 2 * early])
    width = flat[0].shape[1]
    pairs = len(offsets) // 2
    wide, wide_x = 2 * SLOTS, 2 * EXTRA
    flat = [pltpu.with_memory_space_constraint(unit, pltpu.VMEM) for unit in flat]
    return pl.pallas_call(
        functools.partial(pick_kernel, offsets, early, sizes, count, local),
        out_shape=[
            pltpu.VMEM((pairs, local * wide + wide_x, 256), BF16),
            pltpu.VMEM((local, pairs * (wide + wide_x), 128), F32),
            pltpu.VMEM((local, early * (wide + wide_x), width), BF16),
        ],
        in_specs=[SMEM, VMEM] + [VMEM] * len(flat),
        out_specs=[VMEM] * 3,
        cost_estimate=pl.CostEstimate(flops=SMALL, transcendentals=0, bytes_accessed=SMALL),
        compiler_params=pltpu.CompilerParams(vmem_limit_bytes=6 << 20),
        name="pick",
    )(where, meta, *flat)


def experts_kernel(offsets, early, sizes, local, buffers, where, sel, scale, rows_e, *refs):
    refs = list(refs)
    units = [[refs.pop(0) for _ in range(size)] for size in sizes]
    ready = [refs.pop(0) for _ in range(3)]
    source = [refs.pop(0) for _ in range(3)]
    outs = [[refs.pop(0) for _ in range(2)] for _ in offsets]
    held = [refs.pop(0) for _ in range(3)]
    eo, rows, sem = refs
    pairs = len(offsets) // 2
    late = pairs - early
    width = rows.shape[2]
    wide, wide_x = 2 * SLOTS, 2 * EXTRA
    base, base_e, base_l = pairs * wide, early * wide, late * wide
    hot = where[1]

    def fetching(e, k):
        at = lax.rem(e - 1, buffers)
        return pltpu.make_async_copy(source[k].at[e], held[k].at[at], sem.at[at, k])

    for e in range(1, min(buffers + 1, local)):
        for k in range(3):
            fetching(e, k).start()

    for p in range(late):
        gather_pair(sel[early + p], units[2 * p] + units[2 * p + 1], rows, p, base_l, local, hot)
    for p in range(pairs):
        eo[p, pl.ds(local * wide, wide_x), :] = jnp.zeros((wide_x, width), BF16)

    def run(e, gates, uppers, downs, before_down, whole):
        tokens = [rows_e[e, :base_e], rows[e, :base_l]]
        if whole:
            tokens += [rows_e[e, base_e:], rows[e, base_l:]]
        tokens = jnp.concatenate(tokens, axis=0)
        gate = dot_t(tokens, gates[...])
        upper = dot_t(tokens, uppers[...])
        weight = scale[e, : tokens.shape[0]][:, :1]
        hidden = (gate / (1.0 + jnp.exp(-gate)) * upper * weight).astype(BF16)
        before_down()
        out = dot(hidden, downs[...]).astype(BF16)
        for p in range(pairs):
            at = e * wide if isinstance(e, int) else pl.multiple_of(e * wide, wide)
            eo[p, pl.ds(at, wide), :] = out[p * wide : (p + 1) * wide]
            if whole:
                eo[p, pl.ds(local * wide, wide_x), :] = out[base + p * wide_x : base + (p + 1) * wide_x]

    def either(e, *rest):
        @pl.when(hot == e)
        def _():
            run(e, *rest, True)

        @pl.when(hot != e)
        def _():
            run(e, *rest, False)

    either(0, *ready, lambda: None)

    def body(e, carry):
        at = lax.rem(e - 1, buffers)
        fetching(e, 0).wait()
        fetching(e, 1).wait()
        either(e, *(w.at[at] for w in held), lambda: fetching(e, 2).wait())

        @pl.when(e + buffers < local)
        def _():
            for k in range(3):
                fetching(e + buffers, k).start()

        return carry

    lax.fori_loop(1, local, body, 0)

    for p in range(pairs):
        total = dot_l(sel[p], eo[p]).astype(BF16)
        for i in range(4):
            outs[2 * p + i // 2][i % 2][...] = total[i * 64 : (i + 1) * 64]


def run_experts(offsets, early, local, where, picked, blocks, ready, weights):
    hidden, width = weights[2].shape[1:]
    wide, wide_x = 2 * SLOTS, 2 * EXTRA
    pairs = len(offsets) // 2
    late = pairs - early
    high = local * wide + wide_x
    full, full_l = pairs * (wide + wide_x), late * (wide + wide_x)
    buffers = max(1, min(local - 1, 2))
    flat = [unit for o in offsets[2 * early :] for unit in blocks[o]]
    sizes = tuple(len(blocks[o]) for o in offsets[2 * early :])
    room = 2 * width * (3 * buffers * hidden + local * full_l + pairs * high)
    room += full * (6 * width + 10 * hidden) + (2 << 20)
    inside = [pltpu.with_memory_space_constraint(v, pltpu.VMEM) for v in [*picked, *flat, *ready]]
    weights = [pltpu.with_memory_space_constraint(w, pltpu.HBM) for w in weights]
    return pl.pallas_call(
        functools.partial(experts_kernel, offsets, early, sizes, local, buffers),
        out_shape=[pltpu.VMEM((64, width), BF16)] * (2 * len(offsets)),
        in_specs=[SMEM] + [VMEM] * len(inside) + [HBM] * 3,
        out_specs=[VMEM] * (2 * len(offsets)),
        scratch_shapes=[
            pltpu.VMEM((buffers, hidden, width), BF16),
            pltpu.VMEM((buffers, hidden, width), BF16),
            pltpu.VMEM((buffers, hidden, width), BF16),
            pltpu.VMEM((pairs, high, width), BF16),
            pltpu.VMEM((local, full_l, width), BF16),
            pltpu.SemaphoreType.DMA((buffers, 3)),
        ],
        cost_estimate=pl.CostEstimate(
            flops=2 * 3 * width * hidden * local * pairs * wide + 4 * len(offsets) * 128 * high * width,
            transcendentals=local * pairs * wide * hidden,
            bytes_accessed=6 * local * hidden * width,
        ),
        compiler_params=pltpu.CompilerParams(vmem_limit_bytes=room),
        name="routed_experts",
    )(where, *inside, *weights)


def shared_kernel(count, *refs):
    blocks, weights, ahead = refs[:count], refs[count : count + 3], refs[count + 3 : count + 6]
    outs, ready = refs[count + 6 : count + 8], refs[count + 8 : count + 11]
    x, wg, wu, wd, out, sem, sem_r = refs[count + 11 :]
    rows = blocks[0].shape[0]
    loads = [
        pltpu.make_async_copy(block, x.at[pl.ds(i * rows, rows)], sem.at[i]) for i, block in enumerate(blocks)
    ]
    loads += [
        pltpu.make_async_copy(source, target, sem.at[count + k])
        for k, (source, target) in enumerate(zip(weights, (wg, wu, wd)))
    ]
    fetches = [
        pltpu.make_async_copy(source.at[0], target, sem_r.at[k])
        for k, (source, target) in enumerate(zip(ahead, ready))
    ]
    for copy in loads:
        copy.start()
    for copy in loads[:-2]:
        copy.wait()
    for copy in fetches:
        copy.start()
    gate = dot(x[...], wg[...])
    loads[-2].wait()
    upper = dot(x[...], wu[...])
    hidden = (gate / (1.0 + jnp.exp(-gate)) * upper).astype(BF16)
    loads[-1].wait()
    half = count * rows // 2
    stores = []
    for i in (1, 0):
        out[i] = dot(hidden[i * half : (i + 1) * half], wd[...]).astype(BF16)
        stores.append(pltpu.make_async_copy(out.at[i], outs[i], sem.at[count + 3 + i]))
        stores[-1].start()
    for copy in fetches + stores:
        copy.wait()


def run_shared(blocks, weights, ahead):
    count = len(blocks)
    rows, width = blocks[0].shape
    hidden = weights[0].shape[1]
    blocks = [pltpu.with_memory_space_constraint(block, pltpu.HBM) for block in blocks]
    weights = [pltpu.with_memory_space_constraint(w, pltpu.HBM) for w in [*weights, *ahead]]
    return pl.pallas_call(
        functools.partial(shared_kernel, count),
        out_shape=[pltpu.HBM((count * rows // 2, width), BF16)] * 2
        + [pltpu.VMEM(w.shape[1:], BF16) for w in ahead],
        in_specs=[HBM] * (count + 6),
        out_specs=[HBM] * 2 + [VMEM] * 3,
        scratch_shapes=[
            pltpu.VMEM((count * rows, width), BF16),
            pltpu.VMEM((width, hidden), BF16),
            pltpu.VMEM((width, hidden), BF16),
            pltpu.VMEM((hidden, width), BF16),
            pltpu.VMEM((2, count * rows // 2, width), BF16),
            pltpu.SemaphoreType.DMA((count + 5,)),
            pltpu.SemaphoreType.DMA((3,)),
        ],
        cost_estimate=pl.CostEstimate(
            flops=SMALL, transcendentals=0, bytes_accessed=SMALL,
        ),
        compiler_params=pltpu.CompilerParams(vmem_limit_bytes=20 << 20),
        name="shared_experts",
    )(*blocks, *weights)


def tied(values, anchors):
    return lax.optimization_barrier((tuple(values), tuple(anchors)))[0]


def on_device(
    latents,
    expert_ids,
    gate_weights,
    capacity,
    hot_expert,
    w_gate,
    w_up,
    w_down,
    shared_gate,
    shared_up,
    shared_down,
):
    tokens, width = latents.shape
    half = tokens // 2
    local = w_gate.shape[0]
    count = lax.axis_size("expert")
    n_dp = lax.axis_size("dp")
    ring = ring_of(count)
    forward = [(ring[i], ring[(i + 1) % count]) for i in range(count)]
    backward = [(b, a) for a, b in forward]
    mid = count // 2

    info = routing(expert_ids, gate_weights, capacity, hot_expert, capacity.shape[1])
    info = info.reshape(count, 2 * local, tokens)
    meta = lax.all_to_all(info, "expert", split_axis=0, concat_axis=0, tiled=True)
    me = lax.axis_index("expert")
    where = jnp.stack([me, hot_expert[0] - me * local]).astype(jnp.int32)
    weights = [jnp.swapaxes(w_gate, 1, 2), jnp.swapaxes(w_up, 1, 2), w_down]

    bits = [1 << b for b in range(n_dp.bit_length() - 1)]
    blocks = {o: [None, None] for o in range(count)}
    up, down = [latents[:half], latents[half:]], [latents[:half], latents[half:]]
    for hop in range(1, mid + 1):
        if hop == mid:
            blocks[0] = [latents]
            order = offsets_of(count)
            order = order[2:-2] + order[-2:] + order[:2]
            picked = run_pick(tuple(order[:8]), 2, count, local, where, meta, blocks)
            up[0], down[1] = tied([up[0], down[1]], [picked[1]])
        for h in range(2):
            if hop < mid or h == 0:
                up[h] = lax.ppermute(up[h], "expert", forward)
                blocks[hop][h] = up[h]
            if hop < mid or h == 1:
                down[h] = lax.ppermute(down[h], "expert", backward)
                blocks[count - hop][h] = down[h]
    mine = [latents]
    for bit in reversed(bits[1:]):
        swap = [(d, d ^ bit) for d in range(n_dp)]
        mine += [lax.ppermute(block, "dp", swap) for block in mine]
    mine = jnp.concatenate(mine, axis=0)
    swap = [(d, d ^ 1) for d in range(n_dp)]
    keep, give, *ready = run_shared(
        [mine, lax.ppermute(mine, "dp", swap)], (shared_gate, shared_up, shared_down), weights
    )
    shared = keep.astype(F32) + lax.ppermute(give, "dp", swap).astype(F32)
    turns = [0]
    for bit in reversed(bits[1:]):
        turns += [r ^ bit for r in turns]
    part = {r: shared[i * tokens : (i + 1) * tokens] for i, r in enumerate(turns)}
    for bit in bits[1:]:
        swap = [(d, d ^ bit) for d in range(n_dp)]
        for r in sorted(part):
            if r & bit:
                came = lax.ppermute(part.pop(r).astype(BF16), "dp", swap)
                part[r ^ bit] = part[r ^ bit] + came.astype(F32)
    shared = part[0]

    done = {}
    for at in range(0, count, 8):
        chunk = tuple(order[at : at + 8])
        if at > 0:
            picked = run_pick(chunk, 2, count, local, where, meta, blocks)
        flat = run_experts(chunk, 2, local, where, picked, blocks, ready, weights)
        for i, o in enumerate(chunk):
            done[o] = [flat[2 * i], flat[2 * i + 1]]

    result = []
    for h in range(2):
        pieces = [done[0][h]]
        for step, perm, long in ((-1, forward, h == 0), (1, backward, h == 1)):
            start = mid if long else mid - 1
            acc = done[(step * start) % count][h]
            for k in range(start, 0, -1):
                came = lax.ppermute(acc, "expert", perm)
                if k > 1:
                    acc = (came.astype(F32) + done[(step * (k - 1)) % count][h].astype(F32)).astype(BF16)
            pieces.append(came)
        total = shared[h * half : (h + 1) * half].astype(F32)
        for piece in pieces:
            total = total + piece.astype(F32)
        result.append(total.astype(BF16))
    return jnp.concatenate(result, axis=0)


def solution(mesh):
    placed = (
        P(("dp", "expert"), None),
        P(("dp", "expert"), None),
        P(("dp", "expert"), None),
        P("dp", None),
        P("dp"),
        P("expert", None, None),
        P("expert", None, None),
        P("expert", None, None),
        P(None, "dp"),
        P(None, "dp"),
        P("dp", None),
    )
    return jax.shard_map(
        on_device, mesh=mesh, in_specs=placed, out_specs=P(("dp", "expert"), None), check_vma=False
    )
```

```python
import functools

import jax
import jax.numpy as jnp
from jax import lax
from jax.experimental import pallas as pl
from jax.experimental.pallas import tpu as pltpu
from jax.sharding import PartitionSpec as P

HOT_SLOTS = 40
SLOTS = 24
SMALL = 1000
EXTRA = HOT_SLOTS - SLOTS
BF16 = jnp.bfloat16
F32 = jnp.float32
HBM = pl.BlockSpec(memory_space=pltpu.HBM)
VMEM = pl.BlockSpec(memory_space=pltpu.VMEM)
SMEM = pl.BlockSpec(memory_space=pltpu.SMEM)


def ring_of(count):
    return list(range(0, count, 2)) + list(range(count - 1, 0, -2))


def offsets_of(count):
    order = [0, count // 2]
    for hop in range(1, count // 2):
        order += [hop, count - hop]
    return order


def dot(a, b):
    return jnp.dot(a, b, preferred_element_type=F32)


def dot_t(a, b):
    return lax.dot_general(a, b, (((1,), (1,)), ((), ())), preferred_element_type=F32)


def dot_l(a, b):
    return lax.dot_general(a, b, (((0,), (0,)), ((), ())), preferred_element_type=F32)


def routing(expert_ids, gate_weights, capacity, hot_expert, experts):
    tokens, top = expert_ids.shape
    ids, gates = expert_ids.T, gate_weights.T
    labels = jnp.arange(experts, dtype=jnp.int32)[:, None]
    chosen = jnp.zeros((experts, tokens), jnp.bool_)
    weight = jnp.zeros((experts, tokens), F32)
    for k in range(top):
        here = ids[k][None, :] == labels
        chosen = chosen | here
        weight = weight + jnp.where(here, gates[k][None, :], 0.0)
    place = jnp.arange(tokens, dtype=jnp.int32)
    earlier = (place[:, None] < place[None, :]).astype(BF16)
    rank = dot(chosen.astype(BF16), earlier)
    limit = jnp.where(labels == hot_expert[0], HOT_SLOTS, capacity[0][:, None]).astype(F32)
    kept = chosen & (rank < limit)
    return jnp.stack([jnp.where(kept, rank, -1.0), jnp.where(kept, weight, 0.0)], axis=1)


def source_of(place, offset, count):
    at = jnp.where(place % 2 == 0, place // 2, count // 2 + (count - 1 - place) // 2)
    at = lax.rem(at - offset + count, count)
    return jnp.where(at < count // 2, 2 * at, 2 * count - 1 - 2 * at)


def pick_kernel(offsets, early, sizes, count, local, where, meta, *refs):
    refs = list(refs)
    units = [[refs.pop(0) for _ in range(size)] for size in sizes]
    sel, scale, rows = refs
    pairs = len(offsets) // 2
    wide, wide_x = 2 * SLOTS, 2 * EXTRA
    base, base_e = pairs * wide, early * wide
    hot = where[1]
    lane = lax.broadcasted_iota(jnp.int32, (1, 256), 1)
    second = (lane >= 128).astype(F32)
    for p in range(pairs):
        info = [meta[source_of(where[0], offsets[2 * p + i], count)] for i in range(2)]
        blocks = []
        for e in range(local):
            rank = jnp.concatenate([part[2 * e : 2 * e + 1] for part in info], axis=1)
            gate = jnp.concatenate([part[2 * e + 1 : 2 * e + 2] for part in info], axis=1)
            key = jnp.where((rank >= 0) & (rank < SLOTS), rank + SLOTS * second, -1.0).astype(jnp.int32)
            pick = (lax.broadcasted_iota(jnp.int32, (wide, 256), 0) == key).astype(F32)
            blocks.append(pick)
            scale[e, pl.ds(p * wide, wide), :] = jnp.broadcast_to(
                jnp.sum(pick * gate, axis=1, keepdims=True), (wide, 128)
            )
            key_x = jnp.where((rank >= SLOTS) & (hot == e), rank - SLOTS + EXTRA * second, -1.0)
            pick_x = (lax.broadcasted_iota(jnp.int32, (wide_x, 256), 0) == key_x.astype(jnp.int32)).astype(F32)
            scale[e, pl.ds(base + p * wide_x, wide_x), :] = jnp.broadcast_to(
                jnp.sum(pick_x * gate, axis=1, keepdims=True), (wide_x, 128)
            )
            extra = pick_x if e == 0 else extra + pick_x
        blocks.append(extra)
        sel[p] = jnp.concatenate(blocks, axis=0).astype(BF16)
        if p < early:
            gather_pair(sel[p], units[2 * p] + units[2 * p + 1], rows, p, base_e, local, hot)


def gather_pair(pick, units, rows, p, base, local, hot):
    wide, wide_x = 2 * SLOTS, 2 * EXTRA
    pair = jnp.concatenate([unit[...] for unit in units], axis=0)
    got = dot(pick, pair).astype(BF16)
    for e in range(local):
        rows[e, pl.ds(p * wide, wide), :] = got[e * wide : (e + 1) * wide]

        @pl.when(hot == e)
        def _():
            rows[e, pl.ds(base + p * wide_x, wide_x), :] = got[local * wide :]


def run_pick(offsets, early, count, local, where, meta, blocks):
    flat = [unit for o in offsets[: 2 * early] for unit in blocks[o]]
    sizes = tuple(len(blocks[o]) for o in offsets[: 2 * early])
    width = flat[0].shape[1]
    pairs = len(offsets) // 2
    wide, wide_x = 2 * SLOTS, 2 * EXTRA
    flat = [pltpu.with_memory_space_constraint(unit, pltpu.VMEM) for unit in flat]
    return pl.pallas_call(
        functools.partial(pick_kernel, offsets, early, sizes, count, local),
        out_shape=[
            pltpu.VMEM((pairs, local * wide + wide_x, 256), BF16),
            pltpu.VMEM((local, pairs * (wide + wide_x), 128), F32),
            pltpu.VMEM((local, early * (wide + wide_x), width), BF16),
        ],
        in_specs=[SMEM, VMEM] + [VMEM] * len(flat),
        out_specs=[VMEM] * 3,
        cost_estimate=pl.CostEstimate(flops=SMALL, transcendentals=0, bytes_accessed=SMALL),
        compiler_params=pltpu.CompilerParams(vmem_limit_bytes=6 << 20),
        name="pick",
    )(where, meta, *flat)


def experts_kernel(offsets, early, sizes, local, buffers, where, sel, scale, rows_e, *refs):
    refs = list(refs)
    units = [[refs.pop(0) for _ in range(size)] for size in sizes]
    ready = [refs.pop(0) for _ in range(3)]
    source = [refs.pop(0) for _ in range(3)]
    outs = [[refs.pop(0) for _ in range(2)] for _ in offsets]
    held = [refs.pop(0) for _ in range(3)]
    eo, rows, sem = refs
    pairs = len(offsets) // 2
    late = pairs - early
    width = rows.shape[2]
    wide, wide_x = 2 * SLOTS, 2 * EXTRA
    base, base_e, base_l = pairs * wide, early * wide, late * wide
    hot = where[1]

    def fetching(e, k):
        at = lax.rem(e - 1, buffers)
        return pltpu.make_async_copy(source[k].at[e], held[k].at[at], sem.at[at, k])

    for e in range(1, min(buffers + 1, local)):
        for k in range(3):
            fetching(e, k).start()

    for p in range(late):
        gather_pair(sel[early + p], units[2 * p] + units[2 * p + 1], rows, p, base_l, local, hot)
    for p in range(pairs):
        eo[p, pl.ds(local * wide, wide_x), :] = jnp.zeros((wide_x, width), BF16)

    def run(e, gates, uppers, downs, before_down, whole):
        tokens = [rows_e[e, :base_e], rows[e, :base_l]]
        if whole:
            tokens += [rows_e[e, base_e:], rows[e, base_l:]]
        tokens = jnp.concatenate(tokens, axis=0)
        gate = dot_t(tokens, gates[...])
        upper = dot_t(tokens, uppers[...])
        weight = scale[e, : tokens.shape[0]][:, :1]
        hidden = (gate / (1.0 + jnp.exp(-gate)) * upper * weight).astype(BF16)
        before_down()
        out = dot(hidden, downs[...]).astype(BF16)
        for p in range(pairs):
            at = e * wide if isinstance(e, int) else pl.multiple_of(e * wide, wide)
            eo[p, pl.ds(at, wide), :] = out[p * wide : (p + 1) * wide]
            if whole:
                eo[p, pl.ds(local * wide, wide_x), :] = out[base + p * wide_x : base + (p + 1) * wide_x]

    def either(e, *rest):
        @pl.when(hot == e)
        def _():
            run(e, *rest, True)

        @pl.when(hot != e)
        def _():
            run(e, *rest, False)

    either(0, *ready, lambda: None)

    def body(e, carry):
        at = lax.rem(e - 1, buffers)
        fetching(e, 0).wait()
        fetching(e, 1).wait()
        either(e, *(w.at[at] for w in held), lambda: fetching(e, 2).wait())

        @pl.when(e + buffers < local)
        def _():
            for k in range(3):
                fetching(e + buffers, k).start()

        return carry

    lax.fori_loop(1, local, body, 0)

    for p in range(pairs):
        total = dot_l(sel[p], eo[p]).astype(BF16)
        for i in range(4):
            outs[2 * p + i // 2][i % 2][...] = total[i * 64 : (i + 1) * 64]


def run_experts(offsets, early, local, where, picked, blocks, ready, weights):
    hidden, width = weights[2].shape[1:]
    wide, wide_x = 2 * SLOTS, 2 * EXTRA
    pairs = len(offsets) // 2
    late = pairs - early
    high = local * wide + wide_x
    full, full_l = pairs * (wide + wide_x), late * (wide + wide_x)
    buffers = max(1, min(local - 1, 2))
    flat = [unit for o in offsets[2 * early :] for unit in blocks[o]]
    sizes = tuple(len(blocks[o]) for o in offsets[2 * early :])
    room = 2 * width * (3 * buffers * hidden + local * full_l + pairs * high)
    room += full * (6 * width + 10 * hidden) + (2 << 20)
    inside = [pltpu.with_memory_space_constraint(v, pltpu.VMEM) for v in [*picked, *flat, *ready]]
    weights = [pltpu.with_memory_space_constraint(w, pltpu.HBM) for w in weights]
    return pl.pallas_call(
        functools.partial(experts_kernel, offsets, early, sizes, local, buffers),
        out_shape=[pltpu.VMEM((64, width), BF16)] * (2 * len(offsets)),
        in_specs=[SMEM] + [VMEM] * len(inside) + [HBM] * 3,
        out_specs=[VMEM] * (2 * len(offsets)),
        scratch_shapes=[
            pltpu.VMEM((buffers, hidden, width), BF16),
            pltpu.VMEM((buffers, hidden, width), BF16),
            pltpu.VMEM((buffers, hidden, width), BF16),
            pltpu.VMEM((pairs, high, width), BF16),
            pltpu.VMEM((local, full_l, width), BF16),
            pltpu.SemaphoreType.DMA((buffers, 3)),
        ],
        cost_estimate=pl.CostEstimate(
            flops=2 * 3 * width * hidden * local * pairs * wide + 4 * len(offsets) * 128 * high * width,
            transcendentals=local * pairs * wide * hidden,
            bytes_accessed=6 * local * hidden * width,
        ),
        compiler_params=pltpu.CompilerParams(vmem_limit_bytes=room),
        name="routed_experts",
    )(where, *inside, *weights)


def shared_kernel(count, *refs):
    blocks, weights, ahead = refs[:count], refs[count : count + 3], refs[count + 3 : count + 6]
    outs, ready = refs[count + 6 : count + 8], refs[count + 8 : count + 11]
    x, wg, wu, wd, out, sem, sem_r = refs[count + 11 :]
    rows = blocks[0].shape[0]
    loads = [
        pltpu.make_async_copy(block, x.at[pl.ds(i * rows, rows)], sem.at[i]) for i, block in enumerate(blocks)
    ]
    loads += [
        pltpu.make_async_copy(source, target, sem.at[count + k])
        for k, (source, target) in enumerate(zip(weights, (wg, wu, wd)))
    ]
    fetches = [
        pltpu.make_async_copy(source.at[0], target, sem_r.at[k])
        for k, (source, target) in enumerate(zip(ahead, ready))
    ]
    for copy in loads:
        copy.start()
    for copy in loads[:-2]:
        copy.wait()
    gate = dot(x[...], wg[...])
    loads[-2].wait()
    for copy in fetches:
        copy.start()
    upper = dot(x[...], wu[...])
    hidden = (gate / (1.0 + jnp.exp(-gate)) * upper).astype(BF16)
    loads[-1].wait()
    half = count * rows // 2
    stores = []
    for i in (1, 0):
        out[i] = dot(hidden[i * half : (i + 1) * half], wd[...]).astype(BF16)
        stores.append(pltpu.make_async_copy(out.at[i], outs[i], sem.at[count + 3 + i]))
        stores[-1].start()
    for copy in fetches + stores:
        copy.wait()


def run_shared(blocks, weights, ahead):
    count = len(blocks)
    rows, width = blocks[0].shape
    hidden = weights[0].shape[1]
    blocks = [pltpu.with_memory_space_constraint(block, pltpu.HBM) for block in blocks]
    weights = [pltpu.with_memory_space_constraint(w, pltpu.HBM) for w in [*weights, *ahead]]
    return pl.pallas_call(
        functools.partial(shared_kernel, count),
        out_shape=[pltpu.HBM((count * rows // 2, width), BF16)] * 2
        + [pltpu.VMEM(w.shape[1:], BF16) for w in ahead],
        in_specs=[HBM] * (count + 6),
        out_specs=[HBM] * 2 + [VMEM] * 3,
        scratch_shapes=[
            pltpu.VMEM((count * rows, width), BF16),
            pltpu.VMEM((width, hidden), BF16),
            pltpu.VMEM((width, hidden), BF16),
            pltpu.VMEM((hidden, width), BF16),
            pltpu.VMEM((2, count * rows // 2, width), BF16),
            pltpu.SemaphoreType.DMA((count + 5,)),
            pltpu.SemaphoreType.DMA((3,)),
        ],
        cost_estimate=pl.CostEstimate(
            flops=SMALL, transcendentals=0, bytes_accessed=SMALL,
        ),
        compiler_params=pltpu.CompilerParams(vmem_limit_bytes=20 << 20),
        name="shared_experts",
    )(*blocks, *weights)


def tied(values, anchors):
    return lax.optimization_barrier((tuple(values), tuple(anchors)))[0]


def on_device(
    latents,
    expert_ids,
    gate_weights,
    capacity,
    hot_expert,
    w_gate,
    w_up,
    w_down,
    shared_gate,
    shared_up,
    shared_down,
):
    tokens, width = latents.shape
    half = tokens // 2
    local = w_gate.shape[0]
    count = lax.axis_size("expert")
    n_dp = lax.axis_size("dp")
    ring = ring_of(count)
    forward = [(ring[i], ring[(i + 1) % count]) for i in range(count)]
    backward = [(b, a) for a, b in forward]
    mid = count // 2

    info = routing(expert_ids, gate_weights, capacity, hot_expert, capacity.shape[1])
    info = info.reshape(count, 2 * local, tokens)
    meta = lax.all_to_all(info, "expert", split_axis=0, concat_axis=0, tiled=True)
    me = lax.axis_index("expert")
    where = jnp.stack([me, hot_expert[0] - me * local]).astype(jnp.int32)
    weights = [jnp.swapaxes(w_gate, 1, 2), jnp.swapaxes(w_up, 1, 2), w_down]

    bits = [1 << b for b in range(n_dp.bit_length() - 1)]
    blocks = {o: [None, None] for o in range(count)}
    up, down = [latents[:half], latents[half:]], [latents[:half], latents[half:]]
    for hop in range(1, mid + 1):
        if hop == mid:
            blocks[0] = [latents]
            order = offsets_of(count)
            order = order[2:-2] + order[-2:] + order[:2]
            picked = run_pick(tuple(order[:8]), 2, count, local, where, meta, blocks)
            up[0], down[1] = tied([up[0], down[1]], [picked[1]])
        for h in range(2):
            if hop < mid or h == 0:
                up[h] = lax.ppermute(up[h], "expert", forward)
                blocks[hop][h] = up[h]
            if hop < mid or h == 1:
                down[h] = lax.ppermute(down[h], "expert", backward)
                blocks[count - hop][h] = down[h]
    mine = [latents]
    for bit in reversed(bits[1:]):
        swap = [(d, d ^ bit) for d in range(n_dp)]
        mine += [lax.ppermute(block, "dp", swap) for block in mine]
    mine = jnp.concatenate(mine, axis=0)
    swap = [(d, d ^ 1) for d in range(n_dp)]
    keep, give, *ready = run_shared(
        [mine, lax.ppermute(mine, "dp", swap)], (shared_gate, shared_up, shared_down), weights
    )
    shared = keep.astype(F32) + lax.ppermute(give, "dp", swap).astype(F32)
    turns = [0]
    for bit in reversed(bits[1:]):
        turns += [r ^ bit for r in turns]
    part = {r: shared[i * tokens : (i + 1) * tokens] for i, r in enumerate(turns)}
    for bit in bits[1:]:
        swap = [(d, d ^ bit) for d in range(n_dp)]
        for r in sorted(part):
            if r & bit:
                came = lax.ppermute(part.pop(r).astype(BF16), "dp", swap)
                part[r ^ bit] = part[r ^ bit] + came.astype(F32)
    shared = part[0]

    done = {}
    for at in range(0, count, 8):
        chunk = tuple(order[at : at + 8])
        if at > 0:
            picked = run_pick(chunk, 2, count, local, where, meta, blocks)
        flat = run_experts(chunk, 2, local, where, picked, blocks, ready, weights)
        for i, o in enumerate(chunk):
            done[o] = [flat[2 * i], flat[2 * i + 1]]

    result = []
    for h in range(2):
        pieces = [done[0][h]]
        for step, perm, long in ((-1, forward, h == 0), (1, backward, h == 1)):
            start = mid if long else mid - 1
            acc = done[(step * start) % count][h]
            for k in range(start, 0, -1):
                came = lax.ppermute(acc, "expert", perm)
                if k > 1:
                    acc = (came.astype(F32) + done[(step * (k - 1)) % count][h].astype(F32)).astype(BF16)
            pieces.append(came)
        total = shared[h * half : (h + 1) * half].astype(F32)
        for piece in pieces:
            total = total + piece.astype(F32)
        result.append(total.astype(BF16))
    return jnp.concatenate(result, axis=0)


def solution(mesh):
    placed = (
        P(("dp", "expert"), None),
        P(("dp", "expert"), None),
        P(("dp", "expert"), None),
        P("dp", None),
        P("dp"),
        P("expert", None, None),
        P("expert", None, None),
        P("expert", None, None),
        P(None, "dp"),
        P(None, "dp"),
        P("dp", None),
    )
    return jax.shard_map(
        on_device, mesh=mesh, in_specs=placed, out_specs=P(("dp", "expert"), None), check_vma=False
    )
```
